512 devices in a mesh: mx: 16 (over y, z_hi), my: 16 (over x, z_lo), dz: 2 (over core).
Axes of the slice: x: 4, y: 4, z: 16 (z_hi: 4, z_lo: 4; z = z_hi * 4 + z_lo), core: 2. Of those that a mesh axis runs over, the one named last changes fastest.
Arguments:
- electric: float32 [3, 16, 256, 2048], P(None, 'dz', 'mx', 'my'), may hold values from -6 to 6
- magnetic: float32 [3, 16, 256, 2048], P(None, 'dz', 'mx', 'my'), may hold values from -6 to 6
- poles: float32 [3, 3, 16, 256, 2048], P(None, None, 'dz', 'mx', 'my'), may hold values from -4 to 4
- material: int32 [16, 256, 2048], P('dz', 'mx', 'my'), may hold values from 0 to 3
- exit_layer: int32 [1], replicated, may hold values from 0 to 15
Outputs:
- electric_next: float32 [3, 16, 256, 2048], P(None, 'dz', 'mx', 'my')
- magnetic_next: float32 [3, 16, 256, 2048], P(None, 'dz', 'mx', 'my')
- poles_next: float32 [3, 3, 16, 256, 2048], P(None, None, 'dz', 'mx', 'my')
- far_field: float32 [4, 2, 2, 128, 128], P('dz', None, None, 'mx', 'my')
The draws below stay inside these ranges and needn't reach their ends.
All inputs are finite; a program needn't handle non-finite values.
Results may differ from the reference program's by a relative error of at most 0.00016.
Values sent between devices are 32-bit elements; how exact they have to be, the bound alone decides.
A program may use at most 64 MiB of HBM per device.

```python
import math
import jax
import jax.numpy as jnp
import numpy as np
from jax import lax

STEPS = 4
W = 4
U = 128
V = 128
NX = 256
NY = 2048
NZ = 16


def place_ends(drawn, stream_key, least, largest):
    spot = [jax.random.randint(jax.random.fold_in(stream_key, axis), (), 0, length) for axis, length in enumerate(drawn.shape)]
    longest = drawn.shape.index(max(drawn.shape))
    neighbour = spot[:longest] + [(spot[longest] + 1) % drawn.shape[longest]] + spot[longest + 1:]
    return drawn.at[tuple(spot)].set(least).at[tuple(neighbour)].set(largest)


def steps_of(rng, extent, pieces, low, top_value):
    factor_of, own = 1.0, jax.random.fold_in(rng, 6)
    for axis_at, blocks in pieces:
        draws = jnp.exp(jax.random.uniform(jax.random.fold_in(own, axis_at), (blocks,), jnp.float32, low / len(pieces), top_value / len(pieces)))
        factor_of = factor_of * jnp.repeat(draws, extent[axis_at] // blocks).reshape([-1 if axis == axis_at else 1 for axis in range(len(extent))])
    return factor_of


def gaussian(rng, extent, deviation, most, shards=(), dtype=jnp.bfloat16):
    values = jax.random.normal(rng, extent, jnp.float32) * deviation
    if len(shards) > 0:
        values = steps_of(rng, extent, shards, -0.22, 0.18) * values
    return jnp.clip(values, min=-most, max=most).astype(dtype)


def setup_inputs(seed: int = 0) -> dict:
    key_list = jax.random.split(jax.random.key(seed), 6)
    return {
        "electric": gaussian(key_list[0], (3, NZ, NX, NY), 1.0, 6.0, ((1, 2), (2, 16), (3, 16)), jnp.float32),
        "magnetic": gaussian(key_list[1], (3, NZ, NX, NY), 1.0, 6.0, ((1, 2), (2, 16), (3, 16)), jnp.float32),
        "poles": gaussian(key_list[2], (3, 3, NZ, NX, NY), 0.5, 4.0, ((2, 2), (3, 16), (4, 16)), jnp.float32),
        "material": place_ends(jax.random.randint(key_list[3], (NZ, NX, NY), 0, 4), jax.random.fold_in(key_list[3], 1), 0, 3).astype(jnp.int32),
        "exit_layer": jax.random.randint(key_list[4], (1,), 0, NZ).astype(jnp.int32),
    }


time_step = 0.5
eps_inf = np.array([1.0, 4.0, 2.1, 1.5])
drude_plasma = np.array([0.0, 0.0, 0.0, 2.0])
drude_damping = np.array([0.0, 0.0, 0.0, 0.1])
lorentz_square = np.array([0.3, 0.8, 1.0, 0.5])
lorentz_strength = np.array([0.0, 1.5, 0.1, 0.8])
lorentz_damping = np.array([0.0, 0.05, 0.02, 0.2])
drude_keep = (1.0 - drude_damping * time_step / 2) / (1.0 + drude_damping * time_step / 2)
drude_drive = drude_plasma * time_step / (1.0 + drude_damping * time_step / 2)
lorentz_keep = (1.0 - lorentz_damping * time_step / 2) / (1.0 + lorentz_damping * time_step / 2)
lorentz_push = time_step / (1.0 + lorentz_damping * time_step / 2)
coef_table = np.stack([drude_keep, drude_drive, lorentz_keep, lorentz_push * lorentz_square * lorentz_strength, lorentz_push * lorentz_square, time_step / eps_inf]).astype(np.float32)

def coefficients(material):
    result = []
    for row in range(6):
        value = jnp.zeros(material.shape, jnp.float32)
        for which in range(4):
            value = value + jnp.where(material == which, jnp.float32(coef_table[row, which]), jnp.float32(0.0))
        result.append(value)
    return result

def forward(field, axis):
    inner = lax.slice_in_dim(field, 1, field.shape[axis], axis=axis)
    zeros = jnp.zeros_like(lax.slice_in_dim(field, 0, 1, axis=axis))
    return jnp.concatenate([inner, zeros], axis) - field

def backward(field, axis):
    inner = lax.slice_in_dim(field, 0, field.shape[axis] - 1, axis=axis)
    zeros = jnp.zeros_like(lax.slice_in_dim(field, 0, 1, axis=axis))
    return field - jnp.concatenate([zeros, inner], axis)

def curl_of(field, differ):
    part_x, part_y, part_z = (field[0], field[1], field[2])
    return jnp.stack([differ(part_z, 2) - differ(part_y, 0), differ(part_x, 0) - differ(part_z, 1), differ(part_y, 1) - differ(part_x, 2)])

def phase_tables(waves, total_steps):
    period = (8 + 2 * waves).astype(jnp.float32)
    moments = jnp.arange(1, total_steps + 1).astype(jnp.float32)
    angle = 2 * math.pi * moments[None, :] / period[:, None]
    return (jnp.cos(angle), jnp.sin(angle))

def transform_table(waves, outputs, positions, center, scale):
    rows = jnp.arange(outputs).astype(jnp.int32) - outputs // 2
    product = rows[:, None] * (positions - center)[None, :]
    period = outputs * (5 + waves)
    folded = jnp.mod(product[None, :, :], period[:, None, None])
    angle = 2 * math.pi * folded.astype(jnp.float32) / period.astype(jnp.float32)[:, None, None]
    return (scale * jnp.cos(angle), -scale * jnp.sin(angle))

def product_of(form, left, right):
    return jnp.einsum(form, left, right, precision=lax.Precision.HIGHEST)

def along_rows(kern_re, kern_im, data_re, data_im):
    form = 'wux,wpxy->wpuy'
    real = product_of(form, kern_re, data_re) - product_of(form, kern_im, data_im)
    imag = product_of(form, kern_re, data_im) + product_of(form, kern_im, data_re)
    return (real, imag)

def along_columns(data_re, data_im, kern_re, kern_im):
    form = 'wpuy,wvy->wpuv'
    real = product_of(form, data_re, kern_re) - product_of(form, data_im, kern_im)
    imag = product_of(form, data_im, kern_re) + product_of(form, data_re, kern_im)
    return (real, imag)

def reference(electric, magnetic, poles, material, exit_layer):
    keep_d, drive_d, keep_l, drive_l, restore_l, scale_e = coefficients(material)
    polar, current, drude = (poles[0], poles[1], poles[2])
    planes = []
    for _ in range(STEPS):
        magnetic = magnetic - time_step * curl_of(electric, forward)
        current_new = keep_l * current + drive_l * electric - restore_l * polar
        polar = polar + time_step * current_new
        drude_new = keep_d * drude + drive_d * electric
        electric = electric + scale_e * (curl_of(magnetic, backward) - 0.5 * (drude + drude_new) - current_new)
        current, drude = (current_new, drude_new)
        planes.append(lax.dynamic_index_in_dim(electric[:2], exit_layer[0], axis=1, keepdims=False))
    planes = jnp.stack(planes)
    waves = jnp.arange(W).astype(jnp.int32)
    cos_t, sin_t = phase_tables(waves, STEPS)
    phase_re = product_of('wn,npxy->wpxy', cos_t, planes)
    phase_im = -product_of('wn,npxy->wpxy', sin_t, planes)
    row_re, row_im = transform_table(waves, U, jnp.arange(NX).astype(jnp.int32), NX // 2, 1.0 / math.sqrt(NX))
    col_re, col_im = transform_table(waves, V, jnp.arange(NY).astype(jnp.int32), NY // 2, 1.0 / math.sqrt(NY))
    mid_re, mid_im = along_rows(row_re, row_im, phase_re, phase_im)
    far_re, far_im = along_columns(mid_re, mid_im, col_re, col_im)
    far_field = jnp.stack([far_re, far_im], 1)
    poles_next = jnp.stack([polar, current, drude])
    return (electric, magnetic, poles_next, far_field)
```

```python
import functools
import math

import jax
import jax.numpy as jnp
import numpy as np
from jax import lax
from jax.experimental import pallas as pl
from jax.experimental.pallas import tpu as pltpu
from jax.sharding import PartitionSpec as P

STEPS = 4
W = 4
U = 128
V = 128
MESH = pl.DeviceIdType.MESH
F32 = jnp.float32

time_step = 0.5
eps_inf = np.array([1.0, 4.0, 2.1, 1.5])
drude_plasma = np.array([0.0, 0.0, 0.0, 2.0])
drude_damping = np.array([0.0, 0.0, 0.0, 0.1])
lorentz_square = np.array([0.3, 0.8, 1.0, 0.5])
lorentz_strength = np.array([0.0, 1.5, 0.1, 0.8])
lorentz_damping = np.array([0.0, 0.05, 0.02, 0.2])
drude_keep = (1.0 - drude_damping * time_step / 2) / (1.0 + drude_damping * time_step / 2)
drude_drive = drude_plasma * time_step / (1.0 + drude_damping * time_step / 2)
lorentz_keep = (1.0 - lorentz_damping * time_step / 2) / (1.0 + lorentz_damping * time_step / 2)
lorentz_push = time_step / (1.0 + lorentz_damping * time_step / 2)
coef_table = np.stack(
    [
        drude_keep,
        drude_drive,
        lorentz_keep,
        lorentz_push * lorentz_square * lorentz_strength,
        lorentz_push * lorentz_square,
        time_step / eps_inf,
    ]
).astype(np.float32)
DT = np.float32(time_step)

COS_TERMS = [np.float32((-1) ** k * (2 * math.pi) ** (2 * k) / math.factorial(2 * k)) for k in range(11)]
SIN_TERMS = [np.float32((-1) ** k * (2 * math.pi) ** (2 * k + 1) / math.factorial(2 * k + 1)) for k in range(11)]


def poly(terms, z):
    value = jnp.full_like(z, terms[-1])
    for term in terms[-2::-1]:
        value = value * z + term
    return value


def cos_turn(t):
    return poly(COS_TERMS, t * t)


def sin_turn(t):
    return t * poly(SIN_TERMS, t * t)


def fold(product, period, inverse):
    left = product - jnp.floor(product * inverse + 0.5) * period
    return left * inverse


def kernel(
    nmx, nmy,
    e_in, h_in, p_in, m_in, exit_ref,
    e_out, h_out, p_out, f_out,
    e, h, hp, eb, pq, mat, coef,
    xs, ys, zs, ps, xdn, xup, xz, ydn, yup, yz, xy1, xy2, zr, pr,
    rmat, bw, tt, ff, cbuf, ra, gbuf, gall, fbuf,
    in_sem, out_sem, s_send, s_recv, a_send, a_recv, b_send, b_recv,
):
    depth, cx, cy = mat.shape
    steps = xs.shape[0]
    mx, my, dz = lax.axis_index("mx"), lax.axis_index("my"), lax.axis_index("dz")
    side = 2 * dz - 1
    near_x, near_y = lax.rem(mx + side + nmx, nmx), lax.rem(my + side + nmy, nmy)
    up_x, down_x = lax.rem(mx + 1, nmx), lax.rem(mx + nmx - 1, nmx)
    up_y, down_y = lax.rem(my + 1, nmy), lax.rem(my + nmy - 1, nmy)

    loads = [
        pltpu.make_async_copy(src, dst, in_sem.at[i])
        for i, (src, dst) in enumerate(((m_in, mat), (e_in, e), (h_in, h), (p_in, pq)))
    ]
    for load in loads:
        load.start()

    barrier = pltpu.get_barrier_semaphore()
    peers = [(lax.rem(mx + k, nmx), my, dz) for k in range(1, nmx)]
    peers += [(mx, lax.rem(my + k, nmy), dz) for k in range(1, nmy)]
    peers += [(mx, my, 1 - dz), (near_x, my, 1 - dz), (mx, near_y, 1 - dz)]
    peers += [(up_x, down_y, dz), (down_x, up_y, dz)]
    for peer in peers:
        pl.semaphore_signal(barrier, inc=1, device_id=peer, device_id_type=MESH)

    one, zero = np.float32(1.0), np.float32(0.0)
    has_xp, has_xm = jnp.where(mx < nmx - 1, one, zero), jnp.where(mx > 0, one, zero)
    has_yp, has_ym = jnp.where(my < nmy - 1, one, zero), jnp.where(my > 0, one, zero)
    has_zp, has_zm = jnp.where(dz == 0, one, zero), jnp.where(dz == 0, zero, one)
    gx, gy, gz = DT * has_xp, DT * has_yp, DT * has_zp

    lane = lax.broadcasted_iota(jnp.int32, (cx, cy), 1)
    row = lax.broadcasted_iota(jnp.int32, (cx, cy), 0)
    lane1 = lax.broadcasted_iota(jnp.int32, (1, cy), 1)
    at_lane0, at_lane_end = lane == 0, lane == cy - 1
    at_row0, at_row_end = row == 0, row == cx - 1
    end1 = lane1 == cy - 1

    def to(x, src, dst):
        shift = (dst - src) % cy
        return pltpu.roll(x, shift, axis=1) if shift else x

    def y_next(x):
        return pltpu.roll(x, cy - 1, axis=1)

    def y_last(x):
        return pltpu.roll(x, 1, axis=1)

    def x_next(x):
        return pltpu.roll(x, cx - 1, axis=0)

    def x_last(x):
        return pltpu.roll(x, 1, axis=0)

    nothing = jnp.zeros((cx, cy), F32)

    def partial_magnetic(s):
        packed = nothing
        for z in range(depth):
            ex, ey, ez = e[0, z], e[1, z], e[2, z]
            exn, eyn = (e[0, z + 1], e[1, z + 1]) if z + 1 < depth else (nothing, nothing)
            dy_ez = jnp.where(at_lane_end, nothing, y_next(ez)) - ez
            dy_ex = jnp.where(at_lane_end, nothing, y_next(ex)) - ex
            dx_ez = jnp.where(at_row_end, nothing, x_next(ez)) - ez
            dx_ey = jnp.where(at_row_end, nothing, x_next(ey)) - ey
            hx = h[0, z] - DT * (dy_ez - (eyn - ey))
            hy = h[1, z] - DT * ((exn - ex) - dx_ez)
            hz = h[2, z] - DT * (dx_ey - dy_ex)
            hp[0, z], hp[1, z], hp[2, z] = hx, hy, hz
            xs[s, 0, z : z + 1, :] = ey[0:1]
            xs[s, 1, z : z + 1, :] = ez[0:1]
            xs[s, 2, z : z + 1, :] = hy[cx - 1 : cx]
            xs[s, 3, z : z + 1, :] = hz[cx - 1 : cx]
            xs[s, 4, z : z + 1, :] = ex[cx - 1 : cx]
            for which, (x, src) in enumerate(((ex, 0), (ez, 0), (ey, cy - 1), (hx, cy - 1), (hz, cy - 1))):
                at = which * depth + z
                packed = jnp.where(lane == at, to(x, src, at), packed)
            if z == 0:
                low = (ex, ey)
            if z == depth - 1:
                high = (hx, hy)
        ys[s, 0], ys[s, 1] = packed[0:8], packed[8:16]
        for c in range(2):
            zs[s, c] = high[c] * has_zp + low[c] * has_zm

    def message(s, k, src, dst, device):
        return pltpu.make_async_remote_copy(
            src_ref=src, dst_ref=dst, send_sem=s_send.at[s, k], recv_sem=s_recv.at[s, k],
            device_id=device, device_id_type=MESH,
        )

    def plane_message(s):
        return message(s, 9, ps.at[s], pr.at[s], (mx, my, 1 - dz))

    def messages(s):
        return [
            message(s, 0, xs.at[s, pl.ds(0, 2)], xdn.at[s], (down_x, my, dz)),
            message(s, 1, xs.at[s, pl.ds(2, 2)], xup.at[s], (up_x, my, dz)),
            message(s, 2, xs.at[s, 1 + 3 * dz], xz.at[s], (near_x, my, 1 - dz)),
            message(s, 3, ys.at[s], ydn.at[s], (mx, down_y, dz)),
            message(s, 4, ys.at[s], yup.at[s], (mx, up_y, dz)),
            message(s, 5, ys.at[s], yz.at[s], (mx, near_y, 1 - dz)),
            message(s, 6, ys.at[s, 1], xy1.at[s], (up_x, down_y, dz)),
            message(s, 7, ys.at[s, 0], xy2.at[s], (down_x, up_y, dz)),
            message(s, 8, zs.at[s], zr.at[s], (mx, my, 1 - dz)),
        ]

    def update_poles():
        for z in range(depth):
            keep_d, drive_d, keep_l, drive_l, restore_l, scale = [coef[i, z] for i in range(6)]
            for c in range(3):
                field, polar, current, drude = e[c, z], pq[0, c, z], pq[1, c, z], pq[2, c, z]
                current_new = keep_l * current + drive_l * field - restore_l * polar
                drude_new = keep_d * drude + drive_d * field
                pq[0, c, z] = polar + DT * current_new
                pq[1, c, z] = current_new
                pq[2, c, z] = drude_new
                eb[c, z] = field - scale * (0.5 * (drude + drude_new) + current_new)

    def finish_step(s):
        from_yp = jnp.concatenate([ydn[s, 0], ydn[s, 1]], 0) * gy
        from_ym = jnp.concatenate([yup[s, 0], yup[s, 1]], 0)
        edge_yz = jnp.concatenate([yz[s, 0], yz[s, 1]], 0)
        edge_xp = jnp.concatenate([nothing[0:8], pltpu.roll(xy2[s], 7, axis=0)], 0) * gx
        edge_xp = jnp.where(at_row_end, edge_xp, nothing)
        edge_xm = xy1[s, 7:8, :] * gy
        plane = [nothing, nothing]
        hx_below = hy_below = None
        for z in range(depth):
            ex, ey, ez = e[0, z], e[1, z], e[2, z]
            hx, hy, hz = hp[0, z], hp[1, z], hp[2, z]
            ey_xp, ez_xp = xdn[s, 0, z : z + 1, :] * gx, xdn[s, 1, z : z + 1, :] * gx
            hy = hy + jnp.where(at_row_end, jnp.broadcast_to(ez_xp, (cx, cy)), nothing)
            hz = hz - jnp.where(at_row_end, jnp.broadcast_to(ey_xp, (cx, cy)), nothing)
            hx = hx - jnp.where(at_lane_end, to(from_yp, depth + z, cy - 1), nothing)
            hz = hz + jnp.where(at_lane_end, to(from_yp, z, cy - 1), nothing)
            hy_xm = xup[s, 0, z : z + 1, :] + DT * ez[0:1]
            hz_xm = xup[s, 1, z : z + 1, :] - DT * ey[0:1] + jnp.where(end1, to(edge_xm, z, cy - 1), zero)
            hx_ym = to(from_ym, 3 * depth + z, 0) - DT * ez
            hz_ym = to(from_ym, 4 * depth + z, 0) + DT * ex - to(edge_xp, 2 * depth + z, 0)
            if z == depth - 1:
                hx = hx + gz * zr[s, 1]
                hy = hy - gz * zr[s, 0]
                hy_xm = hy_xm - gz * xz[s, 0:1, :]
                hx_ym = hx_ym + gz * to(edge_yz, 2 * depth, 0)
            if z == 0:
                hx_below = zr[s, 0] + DT * ey
                hx_below = hx_below - jnp.where(at_lane_end, gy * to(edge_yz, 2 * depth - 1, cy - 1), nothing)
                hy_below = zr[s, 1] - DT * ex
                hy_below = hy_below + jnp.where(at_row_end, jnp.broadcast_to(xz[s, 7:8, :] * gx, (cx, cy)), nothing)
                hx_below, hy_below = hx_below * has_zm, hy_below * has_zm
            h[0, z], h[1, z], h[2, z] = hx, hy, hz
            dx_hy = hy - jnp.where(at_row0, jnp.broadcast_to(hy_xm * has_xm, (cx, cy)), x_last(hy))
            dx_hz = hz - jnp.where(at_row0, jnp.broadcast_to(hz_xm * has_xm, (cx, cy)), x_last(hz))
            dy_hx = hx - jnp.where(at_lane0, hx_ym * has_ym, y_last(hx))
            dy_hz = hz - jnp.where(at_lane0, hz_ym * has_ym, y_last(hz))
            scale = coef[5, z]
            ex_new = eb[0, z] + scale * (dy_hz - (hy - hy_below))
            ey_new = eb[1, z] + scale * ((hx - hx_below) - dx_hz)
            e[0, z] = ex_new
            e[1, z] = ey_new
            e[2, z] = eb[2, z] + scale * (dx_hy - dy_hx)
            here = jnp.where(depth * dz + z == exit_ref[0], one, zero)
            plane = [plane[0] + here * ex_new, plane[1] + here * ey_new]
            hx_below, hy_below = hx, hy
        ps[s, 0], ps[s, 1] = plane

    dzf, mxf, myf = dz.astype(F32), mx.astype(F32), my.astype(F32)
    vrow = lax.broadcasted_iota(jnp.int32, (V, cy), 0).astype(F32) - np.float32(V // 2)
    ypos = lax.broadcasted_iota(jnp.int32, (V, cy), 1).astype(F32) + (myf - np.float32(nmy // 2)) * np.float32(cy)
    for wl in range(2):
        period = np.float32(V) * (np.float32(5 + wl) + 2 * dzf)
        inverse = jnp.where(dz == 0, np.float32(1.0 / (V * (5 + wl))), np.float32(1.0 / (V * (7 + wl))))
        turn = fold(vrow * ypos, period, inverse)
        size = np.float32(1.0 / math.sqrt(nmy * cy))
        bw[wl, :, 0:cy] = size * cos_turn(turn)
        bw[wl, :, cy : 2 * cy] = -size * sin_turn(turn)

    r = lax.broadcasted_iota(jnp.int32, (128, 128), 0)
    c = lax.broadcasted_iota(jnp.int32, (128, 128), 1)
    w_r, w_c = (r // 32) % 2, c // 64
    own_u = (r % 8).astype(F32) + (mxf * np.float32(8) - np.float32(U // 2))
    inverse = jnp.where(
        w_r == 0,
        jnp.where(dz == 0, np.float32(1.0 / (U * 5)), np.float32(1.0 / (U * 7))),
        jnp.where(dz == 0, np.float32(1.0 / (U * 6)), np.float32(1.0 / (U * 8))),
    )
    quarter = ((r // 16) % 2 - (c // 32) % 2 - r // 64).astype(F32) * np.float32(0.25)
    turn = own_u * (c % 16).astype(F32) * inverse + quarter
    turn = turn - jnp.floor(turn + 0.5)
    same = (w_r == w_c) & ((r // 8) % 2 == (c // 16) % 2)
    tt[...] = jnp.where(same, np.float32(1.0 / math.sqrt(nmx * cx)) * cos_turn(turn), zero)

    width = 8 * nmx
    r = lax.broadcasted_iota(jnp.int32, (64, width), 0)
    c = lax.broadcasted_iota(jnp.int32, (64, width), 1)
    own_u = (r % 8).astype(F32) + (mxf * np.float32(8) - np.float32(U // 2))
    parts = U // cx
    q = (5 + r // 32).astype(F32) + 2 * dzf
    inverse = jnp.where(
        r // 32 == 0,
        jnp.where(dz == 0, np.float32(1.0 / (parts * 5)), np.float32(1.0 / (parts * 7))),
        jnp.where(dz == 0, np.float32(1.0 / (parts * 6)), np.float32(1.0 / (parts * 8))),
    )
    turn = fold(own_u * ((c // 8).astype(F32) - np.float32(nmx // 2)), q * np.float32(parts), inverse)
    ff[0] = cos_turn(turn)
    ff[1] = -sin_turn(turn)

    loads[0].wait()
    for z in range(depth):
        kind = mat[z]
        for i in range(6):
            t = coef_table[i]
            coef[i, z] = jnp.where(kind < 2, jnp.where(kind == 0, t[0], t[1]), jnp.where(kind == 2, t[2], t[3]))
    for load in loads[1:]:
        load.wait()

    partial_magnetic(0)
    pl.semaphore_wait(barrier, len(peers))

    def step(s, carry):
        sent = messages(s)
        for m in sent:
            m.start()
        update_poles()
        for m in sent:
            m.wait()
        finish_step(s)
        plane_message(s).start()

        @pl.when(s + 1 < steps)
        def _():
            partial_magnetic(s + 1)

        return carry

    lax.fori_loop(0, steps, step, 0)

    stores = [
        pltpu.make_async_copy(src, dst, out_sem.at[i])
        for i, (src, dst) in enumerate(((e, e_out), (h, h_out), (pq, p_out)))
    ]
    for store in stores:
        store.start()

    total = [[[nothing, nothing], [nothing, nothing]] for _ in range(2)]
    for s in range(steps):
        plane_message(s).wait()
        for p in range(2):
            plane = ps[s, p] + pr[s, p]
            for wl in range(2):
                angles = [2 * math.pi * (s + 1) / (8 + 2 * (wl + 2 * k)) for k in range(2)]
                cos_t = jnp.where(dz == 0, np.float32(math.cos(angles[0])), np.float32(math.cos(angles[1])))
                sin_t = jnp.where(dz == 0, np.float32(math.sin(angles[0])), np.float32(math.sin(angles[1])))
                total[wl][0][p] = total[wl][0][p] + cos_t * plane
                total[wl][1][p] = total[wl][1][p] - sin_t * plane
    columns = []
    for wl in range(2):
        re, im = jnp.concatenate(total[wl][0], 0), jnp.concatenate(total[wl][1], 0)
        rmat[wl, 0 : 2 * cx, 0:cy] = re
        rmat[wl, 0 : 2 * cx, cy : 2 * cy] = -im
        rmat[wl, 2 * cx : 4 * cx, 0:cy] = im
        rmat[wl, 2 * cx : 4 * cx, cy : 2 * cy] = re
        columns.append(
            lax.dot_general(
                bw[wl], rmat[wl], (((1,), (1,)), ((), ())),
                precision=lax.Precision.HIGHEST, preferred_element_type=F32,
            )
        )
    cbuf[...] = jnp.concatenate(columns, 1).reshape(nmy, 8, 128)

    sent = []
    for k in range(1, nmy):
        to_y = lax.rem(my + k, nmy)
        m = pltpu.make_async_remote_copy(
            src_ref=cbuf.at[to_y], dst_ref=ra.at[k], send_sem=a_send.at[k], recv_sem=a_recv.at[k],
            device_id=(mx, to_y, dz), device_id_type=MESH,
        )
        m.start()
        sent.append(m)
    own = cbuf[my]
    for k, m in enumerate(sent):
        m.wait()
        own = own + ra[k + 1]
    gbuf[...] = own
    gall[mx] = own
    sent = []
    for k in range(1, nmx):
        m = pltpu.make_async_remote_copy(
            src_ref=gbuf, dst_ref=gall.at[mx], send_sem=b_send.at[k], recv_sem=b_recv.at[k],
            device_id=(lax.rem(mx + k, nmx), my, dz), device_id_type=MESH,
        )
        m.start()
        sent.append(m)
    for m in sent:
        m.wait()
    both = lax.dot_general(
        tt[...], gall[...].reshape(width, 128), (((1,), (1,)), ((), ())),
        precision=lax.Precision.HIGHEST, preferred_element_type=F32,
    )
    far = both[0:64] * ff[0] + both[64:128] * ff[1]
    shift = 8
    while shift < width:
        far = far + pltpu.roll(far, shift, axis=1)
        shift *= 2
    far = far.reshape(2, 2, 2, 8, width)
    fbuf[...] = far[..., 0:8]
    last = pltpu.make_async_copy(fbuf, f_out, out_sem.at[3])
    last.start()
    for store in stores:
        store.wait()
    last.wait()


def body(nmx, nmy, electric, magnetic, poles, material, exit_layer):
    depth, cx, cy = material.shape
    vm = lambda *shape: pltpu.VMEM(shape, F32)
    dma = lambda *shape: pltpu.SemaphoreType.DMA(shape)
    anywhere = pl.BlockSpec(memory_space=pl.ANY)
    field = (3, depth, cx, cy)
    share = (2, 2, 2, U // nmx, V // nmy)
    n = STEPS
    return pl.pallas_call(
        functools.partial(kernel, nmx, nmy),
        out_shape=(
            jax.ShapeDtypeStruct(field, F32),
            jax.ShapeDtypeStruct(field, F32),
            jax.ShapeDtypeStruct((3, *field), F32),
            jax.ShapeDtypeStruct(share, F32),
        ),
        in_specs=[anywhere] * 4 + [pl.BlockSpec(memory_space=pltpu.SMEM)],
        out_specs=[anywhere] * 4,
        scratch_shapes=[
            vm(*field), vm(*field), vm(*field), vm(*field), vm(3, *field),
            pltpu.VMEM((depth, cx, cy), jnp.int32), vm(6, depth, cx, cy),
            vm(n, 5, depth, cy), vm(n, 2, 8, cy), vm(n, 2, cx, cy), vm(n, 2, cx, cy),
            vm(n, 2, depth, cy), vm(n, 2, depth, cy), vm(n, depth, cy),
            vm(n, 2, 8, cy), vm(n, 2, 8, cy), vm(n, 2, 8, cy), vm(n, 8, cy), vm(n, 8, cy),
            vm(n, 2, cx, cy), vm(n, 2, cx, cy),
            vm(2, 4 * cx, 2 * cy), vm(2, V, 2 * cy), vm(128, 128), vm(2, 64, 8 * nmx),
            vm(nmy, 8, 128), vm(nmy, 8, 128), vm(8, 128), vm(nmx, 8, 128), vm(*share),
            dma(4), dma(4), dma(n, 10), dma(n, 10), dma(nmy), dma(nmy), dma(nmx), dma(nmx),
        ],
        compiler_params=pltpu.CompilerParams(collective_id=0, has_side_effects=True),
    )(electric, magnetic, poles, material, exit_layer)


def solution(mesh):
    nmx, nmy = mesh.shape["mx"], mesh.shape["my"]
    return jax.shard_map(
        functools.partial(body, nmx, nmy),
        mesh=mesh,
        in_specs=(
            P(None, "dz", "mx", "my"),
            P(None, "dz", "mx", "my"),
            P(None, None, "dz", "mx", "my"),
            P("dz", "mx", "my"),
            P(),
        ),
        out_specs=(
            P(None, "dz", "mx", "my"),
            P(None, "dz", "mx", "my"),
            P(None, None, "dz", "mx", "my"),
            P("dz", None, None, "mx", "my"),
        ),
        check_vma=False,
    )
```

```python
import functools
import math

import jax
import jax.numpy as jnp
import numpy as np
from jax import lax
from jax.experimental import pallas as pl
from jax.experimental.pallas import tpu as pltpu
from jax.sharding import PartitionSpec as P

STEPS = 4
W = 4
U = 128
V = 128
MESH = pl.DeviceIdType.MESH
F32 = jnp.float32

time_step = 0.5
eps_inf = np.array([1.0, 4.0, 2.1, 1.5])
drude_plasma = np.array([0.0, 0.0, 0.0, 2.0])
drude_damping = np.array([0.0, 0.0, 0.0, 0.1])
lorentz_square = np.array([0.3, 0.8, 1.0, 0.5])
lorentz_strength = np.array([0.0, 1.5, 0.1, 0.8])
lorentz_damping = np.array([0.0, 0.05, 0.02, 0.2])
drude_keep = (1.0 - drude_damping * time_step / 2) / (1.0 + drude_damping * time_step / 2)
drude_drive = drude_plasma * time_step / (1.0 + drude_damping * time_step / 2)
lorentz_keep = (1.0 - lorentz_damping * time_step / 2) / (1.0 + lorentz_damping * time_step / 2)
lorentz_push = time_step / (1.0 + lorentz_damping * time_step / 2)
coef_table = np.stack(
    [
        drude_keep,
        drude_drive,
        lorentz_keep,
        lorentz_push * lorentz_square * lorentz_strength,
        lorentz_push * lorentz_square,
        time_step / eps_inf,
    ]
).astype(np.float32)
DT = np.float32(time_step)

COS_TERMS = [np.float32((-1) ** k * (2 * math.pi) ** (2 * k) / math.factorial(2 * k)) for k in range(11)]
SIN_TERMS = [np.float32((-1) ** k * (2 * math.pi) ** (2 * k + 1) / math.factorial(2 * k + 1)) for k in range(11)]


def poly(terms, z):
    value = jnp.full_like(z, terms[-1])
    for term in terms[-2::-1]:
        value = value * z + term
    return value


def cos_turn(t):
    return poly(COS_TERMS, t * t)


def sin_turn(t):
    return t * poly(SIN_TERMS, t * t)


def fold(product, period, inverse):
    left = product - jnp.floor(product * inverse + 0.5) * period
    return left * inverse


def kernel(
    nmx, nmy,
    e_in, h_in, p_in, m_in, exit_ref,
    e_out, h_out, p_out, f_out,
    e, h, hp, eb, pq, mat, coef,
    xs, ys, zs, ps, xdn, xup, xz, ydn, yup, yz, xy1, xy2, zr, pr,
    rmat, bw, tt, ff, cbuf, ra, gbuf, gall, fbuf,
    in_sem, out_sem, known, s_send, s_recv, a_send, a_recv, b_send, b_recv,
):
    depth, cx, cy = mat.shape
    steps = xs.shape[0]
    mx, my, dz = lax.axis_index("mx"), lax.axis_index("my"), lax.axis_index("dz")
    side = 2 * dz - 1
    near_x, near_y = lax.rem(mx + side + nmx, nmx), lax.rem(my + side + nmy, nmy)
    up_x, down_x = lax.rem(mx + 1, nmx), lax.rem(mx + nmx - 1, nmx)
    up_y, down_y = lax.rem(my + 1, nmy), lax.rem(my + nmy - 1, nmy)

    loads = [
        pltpu.make_async_copy(src, dst, in_sem.at[i])
        for i, (src, dst) in enumerate(((m_in, mat), (e_in, e), (h_in, h), (p_in, pq)))
    ]
    for load in loads:
        load.start()

    barrier = pltpu.get_barrier_semaphore()
    peers = [(up_x, my, dz), (down_x, my, dz), (mx, up_y, dz), (mx, down_y, dz)]
    peers += [(mx, my, 1 - dz), (near_x, my, 1 - dz), (mx, near_y, 1 - dz)]
    peers += [(up_x, down_y, dz), (down_x, up_y, dz)]
    for peer in peers:
        pl.semaphore_signal(barrier, inc=1, device_id=peer, device_id_type=MESH)

    one, zero = np.float32(1.0), np.float32(0.0)
    has_xp, has_xm = jnp.where(mx < nmx - 1, one, zero), jnp.where(mx > 0, one, zero)
    has_yp, has_ym = jnp.where(my < nmy - 1, one, zero), jnp.where(my > 0, one, zero)
    has_zp, has_zm = jnp.where(dz == 0, one, zero), jnp.where(dz == 0, zero, one)
    gx, gy, gz = DT * has_xp, DT * has_yp, DT * has_zp

    lane = lax.broadcasted_iota(jnp.int32, (cx, cy), 1)
    row = lax.broadcasted_iota(jnp.int32, (cx, cy), 0)
    lane1 = lax.broadcasted_iota(jnp.int32, (1, cy), 1)
    at_lane0, at_lane_end = lane == 0, lane == cy - 1
    at_row0, at_row_end = row == 0, row == cx - 1
    end1 = lane1 == cy - 1

    def to(x, src, dst):
        shift = (dst - src) % cy
        return pltpu.roll(x, shift, axis=1) if shift else x

    def y_next(x):
        return pltpu.roll(x, cy - 1, axis=1)

    def y_last(x):
        return pltpu.roll(x, 1, axis=1)

    def x_next(x):
        return pltpu.roll(x, cx - 1, axis=0)

    def x_last(x):
        return pltpu.roll(x, 1, axis=0)

    nothing = jnp.zeros((cx, cy), F32)

    def partial_magnetic(s):
        packed = nothing
        for z in range(depth):
            ex, ey, ez = e[0, z], e[1, z], e[2, z]
            exn, eyn = (e[0, z + 1], e[1, z + 1]) if z + 1 < depth else (nothing, nothing)
            dy_ez = jnp.where(at_lane_end, nothing, y_next(ez)) - ez
            dy_ex = jnp.where(at_lane_end, nothing, y_next(ex)) - ex
            dx_ez = jnp.where(at_row_end, nothing, x_next(ez)) - ez
            dx_ey = jnp.where(at_row_end, nothing, x_next(ey)) - ey
            hx = h[0, z] - DT * (dy_ez - (eyn - ey))
            hy = h[1, z] - DT * ((exn - ex) - dx_ez)
            hz = h[2, z] - DT * (dx_ey - dy_ex)
            hp[0, z], hp[1, z], hp[2, z] = hx, hy, hz
            xs[s, 0, z : z + 1, :] = ey[0:1]
            xs[s, 1, z : z + 1, :] = ez[0:1]
            xs[s, 2, z : z + 1, :] = hy[cx - 1 : cx]
            xs[s, 3, z : z + 1, :] = hz[cx - 1 : cx]
            xs[s, 4, z : z + 1, :] = ex[cx - 1 : cx]
            for which, (x, src) in enumerate(((ex, 0), (ez, 0), (ey, cy - 1), (hx, cy - 1), (hz, cy - 1))):
                at = which * depth + z
                packed = jnp.where(lane == at, to(x, src, at), packed)
            if z == 0:
                low = (ex, ey)
            if z == depth - 1:
                high = (hx, hy)
        ys[s, 0], ys[s, 1] = packed[0:8], packed[8:16]
        for c in range(2):
            zs[s, c] = high[c] * has_zp + low[c] * has_zm

    def message(s, k, src, dst, device):
        return pltpu.make_async_remote_copy(
            src_ref=src, dst_ref=dst, send_sem=s_send.at[s, k], recv_sem=s_recv.at[s, k],
            device_id=device, device_id_type=MESH,
        )

    def plane_message(s):
        return message(s, 9, ps.at[s], pr.at[s], (mx, my, 1 - dz))

    def messages(s):
        return [
            message(s, 0, xs.at[s, pl.ds(0, 2)], xdn.at[s], (down_x, my, dz)),
            message(s, 1, xs.at[s, pl.ds(2, 2)], xup.at[s], (up_x, my, dz)),
            message(s, 2, xs.at[s, 1 + 3 * dz], xz.at[s], (near_x, my, 1 - dz)),
            message(s, 3, ys.at[s], ydn.at[s], (mx, down_y, dz)),
            message(s, 4, ys.at[s], yup.at[s], (mx, up_y, dz)),
            message(s, 5, ys.at[s], yz.at[s], (mx, near_y, 1 - dz)),
            message(s, 6, ys.at[s, 1], xy1.at[s], (up_x, down_y, dz)),
            message(s, 7, ys.at[s, 0], xy2.at[s], (down_x, up_y, dz)),
            message(s, 8, zs.at[s], zr.at[s], (mx, my, 1 - dz)),
        ]

    def update_poles():
        for z in range(depth):
            keep_d, drive_d, keep_l, drive_l, restore_l, scale = [coef[i, z] for i in range(6)]
            for c in range(3):
                field, polar, current, drude = e[c, z], pq[0, c, z], pq[1, c, z], pq[2, c, z]
                current_new = keep_l * current + drive_l * field - restore_l * polar
                drude_new = keep_d * drude + drive_d * field
                pq[0, c, z] = polar + DT * current_new
                pq[1, c, z] = current_new
                pq[2, c, z] = drude_new
                eb[c, z] = field - scale * (0.5 * (drude + drude_new) + current_new)

    def finish_step(s):
        from_yp = jnp.concatenate([ydn[s, 0], ydn[s, 1]], 0) * gy
        from_ym = jnp.concatenate([yup[s, 0], yup[s, 1]], 0)
        edge_yz = jnp.concatenate([yz[s, 0], yz[s, 1]], 0)
        edge_xp = jnp.concatenate([nothing[0:8], pltpu.roll(xy2[s], 7, axis=0)], 0) * gx
        edge_xp = jnp.where(at_row_end, edge_xp, nothing)
        edge_xm = xy1[s, 7:8, :] * gy
        plane = [nothing, nothing]
        hx_below = hy_below = None
        for z in range(depth):
            ex, ey, ez = e[0, z], e[1, z], e[2, z]
            hx, hy, hz = hp[0, z], hp[1, z], hp[2, z]
            ey_xp, ez_xp = xdn[s, 0, z : z + 1, :] * gx, xdn[s, 1, z : z + 1, :] * gx
            hy = hy + jnp.where(at_row_end, jnp.broadcast_to(ez_xp, (cx, cy)), nothing)
            hz = hz - jnp.where(at_row_end, jnp.broadcast_to(ey_xp, (cx, cy)), nothing)
            hx = hx - jnp.where(at_lane_end, to(from_yp, depth + z, cy - 1), nothing)
            hz = hz + jnp.where(at_lane_end, to(from_yp, z, cy - 1), nothing)
            hy_xm = xup[s, 0, z : z + 1, :] + DT * ez[0:1]
            hz_xm = xup[s, 1, z : z + 1, :] - DT * ey[0:1] + jnp.where(end1, to(edge_xm, z, cy - 1), zero)
            hx_ym = to(from_ym, 3 * depth + z, 0) - DT * ez
            hz_ym = to(from_ym, 4 * depth + z, 0) + DT * ex - to(edge_xp, 2 * depth + z, 0)
            if z == depth - 1:
                hx = hx + gz * zr[s, 1]
                hy = hy - gz * zr[s, 0]
                hy_xm = hy_xm - gz * xz[s, 0:1, :]
                hx_ym = hx_ym + gz * to(edge_yz, 2 * depth, 0)
            if z == 0:
                hx_below = zr[s, 0] + DT * ey
                hx_below = hx_below - jnp.where(at_lane_end, gy * to(edge_yz, 2 * depth - 1, cy - 1), nothing)
                hy_below = zr[s, 1] - DT * ex
                hy_below = hy_below + jnp.where(at_row_end, jnp.broadcast_to(xz[s, 7:8, :] * gx, (cx, cy)), nothing)
                hx_below, hy_below = hx_below * has_zm, hy_below * has_zm
            h[0, z], h[1, z], h[2, z] = hx, hy, hz
            dx_hy = hy - jnp.where(at_row0, jnp.broadcast_to(hy_xm * has_xm, (cx, cy)), x_last(hy))
            dx_hz = hz - jnp.where(at_row0, jnp.broadcast_to(hz_xm * has_xm, (cx, cy)), x_last(hz))
            dy_hx = hx - jnp.where(at_lane0, hx_ym * has_ym, y_last(hx))
            dy_hz = hz - jnp.where(at_lane0, hz_ym * has_ym, y_last(hz))
            scale = coef[5, z]
            ex_new = eb[0, z] + scale * (dy_hz - (hy - hy_below))
            ey_new = eb[1, z] + scale * ((hx - hx_below) - dx_hz)
            e[0, z] = ex_new
            e[1, z] = ey_new
            e[2, z] = eb[2, z] + scale * (dx_hy - dy_hx)
            here = jnp.where(depth * dz + z == exit_ref[0], one, zero)
            plane = [plane[0] + here * ex_new, plane[1] + here * ey_new]
            hx_below, hy_below = hx, hy
        ps[s, 0], ps[s, 1] = plane

    dzf, mxf, myf = dz.astype(F32), mx.astype(F32), my.astype(F32)
    vrow = lax.broadcasted_iota(jnp.int32, (V, cy), 0).astype(F32) - np.float32(V // 2)
    ypos = lax.broadcasted_iota(jnp.int32, (V, cy), 1).astype(F32) + (myf - np.float32(nmy // 2)) * np.float32(cy)
    for wl in range(2):
        period = np.float32(V) * (np.float32(5 + wl) + 2 * dzf)
        inverse = jnp.where(dz == 0, np.float32(1.0 / (V * (5 + wl))), np.float32(1.0 / (V * (7 + wl))))
        turn = fold(vrow * ypos, period, inverse)
        size = np.float32(1.0 / math.sqrt(nmy * cy))
        bw[wl, :, 0:cy] = size * cos_turn(turn)
        bw[wl, :, cy : 2 * cy] = -size * sin_turn(turn)

    r = lax.broadcasted_iota(jnp.int32, (128, 128), 0)
    c = lax.broadcasted_iota(jnp.int32, (128, 128), 1)
    w_r, w_c = (r // 32) % 2, c // 64
    own_u = (r % 8).astype(F32) + (mxf * np.float32(8) - np.float32(U // 2))
    inverse = jnp.where(
        w_r == 0,
        jnp.where(dz == 0, np.float32(1.0 / (U * 5)), np.float32(1.0 / (U * 7))),
        jnp.where(dz == 0, np.float32(1.0 / (U * 6)), np.float32(1.0 / (U * 8))),
    )
    quarter = ((r // 16) % 2 - (c // 32) % 2 - r // 64).astype(F32) * np.float32(0.25)
    turn = own_u * (c % 16).astype(F32) * inverse + quarter
    turn = turn - jnp.floor(turn + 0.5)
    same = (w_r == w_c) & ((r // 8) % 2 == (c // 16) % 2)
    tt[...] = jnp.where(same, np.float32(1.0 / math.sqrt(nmx * cx)) * cos_turn(turn), zero)

    width = 8 * nmx
    r = lax.broadcasted_iota(jnp.int32, (64, width), 0)
    c = lax.broadcasted_iota(jnp.int32, (64, width), 1)
    own_u = (r % 8).astype(F32) + (mxf * np.float32(8) - np.float32(U // 2))
    parts = U // cx
    q = (5 + r // 32).astype(F32) + 2 * dzf
    inverse = jnp.where(
        r // 32 == 0,
        jnp.where(dz == 0, np.float32(1.0 / (parts * 5)), np.float32(1.0 / (parts * 7))),
        jnp.where(dz == 0, np.float32(1.0 / (parts * 6)), np.float32(1.0 / (parts * 8))),
    )
    turn = fold(own_u * ((c // 8).astype(F32) - np.float32(nmx // 2)), q * np.float32(parts), inverse)
    ff[0] = cos_turn(turn)
    ff[1] = -sin_turn(turn)

    loads[0].wait()
    for z in range(depth):
        kind = mat[z]
        for i in range(6):
            t = coef_table[i]
            coef[i, z] = jnp.where(kind < 2, jnp.where(kind == 0, t[0], t[1]), jnp.where(kind == 2, t[2], t[3]))
    for load in loads[1:]:
        load.wait()

    partial_magnetic(0)
    pl.semaphore_wait(barrier, len(peers))

    def step(s, carry):
        sent = messages(s)
        for m in sent:
            m.start()

        @pl.when(s < 3)
        def _():
            far = 1 + s * (s + 1) // 2
            for there in (far, -far):
                pl.semaphore_signal(
                    known.at[0, s], inc=1, device_id=(lax.rem(mx + there + nmx, nmx), my, dz), device_id_type=MESH
                )
                pl.semaphore_signal(
                    known.at[1, s], inc=1, device_id=(mx, lax.rem(my + there + nmy, nmy), dz), device_id_type=MESH
                )

        update_poles()
        for m in sent:
            m.wait()
        finish_step(s)

        @pl.when(s < 3)
        def _():
            pl.semaphore_wait(known.at[0, s], 2)
            pl.semaphore_wait(known.at[1, s], 2)

        plane_message(s).start()

        @pl.when(s + 1 < steps)
        def _():
            partial_magnetic(s + 1)

        return carry

    lax.fori_loop(0, steps, step, 0)

    stores = [
        pltpu.make_async_copy(src, dst, out_sem.at[i])
        for i, (src, dst) in enumerate(((e, e_out), (h, h_out), (pq, p_out)))
    ]
    for store in stores:
        store.start()

    total = [[[nothing, nothing], [nothing, nothing]] for _ in range(2)]
    for s in range(steps):
        plane_message(s).wait()
        for p in range(2):
            plane = ps[s, p] + pr[s, p]
            for wl in range(2):
                angles = [2 * math.pi * (s + 1) / (8 + 2 * (wl + 2 * k)) for k in range(2)]
                cos_t = jnp.where(dz == 0, np.float32(math.cos(angles[0])), np.float32(math.cos(angles[1])))
                sin_t = jnp.where(dz == 0, np.float32(math.sin(angles[0])), np.float32(math.sin(angles[1])))
                total[wl][0][p] = total[wl][0][p] + cos_t * plane
                total[wl][1][p] = total[wl][1][p] - sin_t * plane
    columns = []
    for wl in range(2):
        re, im = jnp.concatenate(total[wl][0], 0), jnp.concatenate(total[wl][1], 0)
        rmat[wl, 0 : 2 * cx, 0:cy] = re
        rmat[wl, 0 : 2 * cx, cy : 2 * cy] = -im
        rmat[wl, 2 * cx : 4 * cx, 0:cy] = im
        rmat[wl, 2 * cx : 4 * cx, cy : 2 * cy] = re
        columns.append(
            lax.dot_general(
                bw[wl], rmat[wl], (((1,), (1,)), ((), ())),
                precision=lax.Precision.HIGHEST, preferred_element_type=F32,
            )
        )
    cbuf[...] = jnp.concatenate(columns, 1).reshape(nmy, 8, 128)

    sent = []
    for k in range(1, nmy):
        to_y = lax.rem(my + k, nmy)
        m = pltpu.make_async_remote_copy(
            src_ref=cbuf.at[to_y], dst_ref=ra.at[k], send_sem=a_send.at[k], recv_sem=a_recv.at[k],
            device_id=(mx, to_y, dz), device_id_type=MESH,
        )
        m.start()
        sent.append(m)
    own = cbuf[my]
    for k, m in enumerate(sent):
        m.wait()
        own = own + ra[k + 1]
    gbuf[...] = own
    gall[mx] = own
    sent = []
    for k in range(1, nmx):
        m = pltpu.make_async_remote_copy(
            src_ref=gbuf, dst_ref=gall.at[mx], send_sem=b_send.at[k], recv_sem=b_recv.at[k],
            device_id=(lax.rem(mx + k, nmx), my, dz), device_id_type=MESH,
        )
        m.start()
        sent.append(m)
    for m in sent:
        m.wait()
    both = lax.dot_general(
        tt[...], gall[...].reshape(width, 128), (((1,), (1,)), ((), ())),
        precision=lax.Precision.HIGHEST, preferred_element_type=F32,
    )
    far = both[0:64] * ff[0] + both[64:128] * ff[1]
    shift = 8
    while shift < width:
        far = far + pltpu.roll(far, shift, axis=1)
        shift *= 2
    far = far.reshape(2, 2, 2, 8, width)
    fbuf[...] = far[..., 0:8]
    last = pltpu.make_async_copy(fbuf, f_out, out_sem.at[3])
    last.start()
    for store in stores:
        store.wait()
    last.wait()


def hand_over(*refs):
    ins, outs, held, sems = refs[:4], refs[4:8], refs[8:12], refs[12]
    first = [pltpu.make_async_copy(a, b, sems.at[0, i]) for i, (a, b) in enumerate(zip(ins, held))]
    then = [pltpu.make_async_copy(a, b, sems.at[1, i]) for i, (a, b) in enumerate(zip(held, outs))]
    for copy in first:
        copy.start()
    for copy, after in zip(first, then):
        copy.wait()
        after.start()
    for after in then:
        after.wait()


def body(nmx, nmy, electric, magnetic, poles, material, exit_layer):
    depth, cx, cy = material.shape
    vm = lambda *shape: pltpu.VMEM(shape, F32)
    dma = lambda *shape: pltpu.SemaphoreType.DMA(shape)
    anywhere = pl.BlockSpec(memory_space=pl.ANY)
    field = (3, depth, cx, cy)
    share = (2, 2, 2, U // nmx, V // nmy)
    n = STEPS
    outs = pl.pallas_call(
        functools.partial(kernel, nmx, nmy),
        out_shape=(
            jax.ShapeDtypeStruct(field, F32),
            jax.ShapeDtypeStruct(field, F32),
            jax.ShapeDtypeStruct((3, *field), F32),
            jax.ShapeDtypeStruct(share, F32),
        ),
        in_specs=[anywhere] * 4 + [pl.BlockSpec(memory_space=pltpu.SMEM)],
        out_specs=[anywhere] * 4,
        scratch_shapes=[
            vm(*field), vm(*field), vm(*field), vm(*field), vm(3, *field),
            pltpu.VMEM((depth, cx, cy), jnp.int32), vm(6, depth, cx, cy),
            vm(n, 5, depth, cy), vm(n, 2, 8, cy), vm(n, 2, cx, cy), vm(n, 2, cx, cy),
            vm(n, 2, depth, cy), vm(n, 2, depth, cy), vm(n, depth, cy),
            vm(n, 2, 8, cy), vm(n, 2, 8, cy), vm(n, 2, 8, cy), vm(n, 8, cy), vm(n, 8, cy),
            vm(n, 2, cx, cy), vm(n, 2, cx, cy),
            vm(2, 4 * cx, 2 * cy), vm(2, V, 2 * cy), vm(128, 128), vm(2, 64, 8 * nmx),
            vm(nmy, 8, 128), vm(nmy, 8, 128), vm(8, 128), vm(nmx, 8, 128), vm(*share),
            dma(4), dma(4), pltpu.SemaphoreType.REGULAR((2, 3)), dma(n, 10), dma(n, 10), dma(nmy), dma(nmy), dma(nmx), dma(nmx),
        ],
        compiler_params=pltpu.CompilerParams(collective_id=0, has_side_effects=True),
    )(electric, magnetic, poles, material, exit_layer)
    shapes = (field, field, (3, *field), share)
    return pl.pallas_call(
        hand_over,
        out_shape=tuple(jax.ShapeDtypeStruct(shape, F32) for shape in shapes),
        in_specs=[anywhere] * 4,
        out_specs=[anywhere] * 4,
        scratch_shapes=[vm(*shape) for shape in shapes] + [dma(2, 4)],
    )(*outs)


def solution(mesh):
    nmx, nmy = mesh.shape["mx"], mesh.shape["my"]
    return jax.shard_map(
        functools.partial(body, nmx, nmy),
        mesh=mesh,
        in_specs=(
            P(None, "dz", "mx", "my"),
            P(None, "dz", "mx", "my"),
            P(None, None, "dz", "mx", "my"),
            P("dz", "mx", "my"),
            P(),
        ),
        out_specs=(
            P(None, "dz", "mx", "my"),
            P(None, "dz", "mx", "my"),
            P(None, None, "dz", "mx", "my"),
            P("dz", None, None, "mx", "my"),
        ),
        check_vma=False,
    )
```

```python
import functools
import math

import jax
import jax.numpy as jnp
import numpy as np
from jax import lax
from jax.experimental import pallas as pl
from jax.experimental.pallas import tpu as pltpu
from jax.sharding import PartitionSpec as P

STEPS = 4
W = 4
U = 128
V = 128
MESH = pl.DeviceIdType.MESH
F32 = jnp.float32

time_step = 0.5
eps_inf = np.array([1.0, 4.0, 2.1, 1.5])
drude_plasma = np.array([0.0, 0.0, 0.0, 2.0])
drude_damping = np.array([0.0, 0.0, 0.0, 0.1])
lorentz_square = np.array([0.3, 0.8, 1.0, 0.5])
lorentz_strength = np.array([0.0, 1.5, 0.1, 0.8])
lorentz_damping = np.array([0.0, 0.05, 0.02, 0.2])
drude_keep = (1.0 - drude_damping * time_step / 2) / (1.0 + drude_damping * time_step / 2)
drude_drive = drude_plasma * time_step / (1.0 + drude_damping * time_step / 2)
lorentz_keep = (1.0 - lorentz_damping * time_step / 2) / (1.0 + lorentz_damping * time_step / 2)
lorentz_push = time_step / (1.0 + lorentz_damping * time_step / 2)
coef_table = np.stack(
    [
        drude_keep,
        drude_drive,
        lorentz_keep,
        lorentz_push * lorentz_square * lorentz_strength,
        lorentz_push * lorentz_square,
        time_step / eps_inf,
    ]
).astype(np.float32)
DT = np.float32(time_step)

COS_TERMS = [np.float32((-1) ** k * (2 * math.pi) ** (2 * k) / math.factorial(2 * k)) for k in range(11)]
SIN_TERMS = [np.float32((-1) ** k * (2 * math.pi) ** (2 * k + 1) / math.factorial(2 * k + 1)) for k in range(11)]


def poly(terms, z):
    value = jnp.full_like(z, terms[-1])
    for term in terms[-2::-1]:
        value = value * z + term
    return value


def cos_turn(t):
    return poly(COS_TERMS, t * t)


def sin_turn(t):
    return t * poly(SIN_TERMS, t * t)


def fold(product, period, inverse):
    left = product - jnp.floor(product * inverse + 0.5) * period
    return left * inverse


def kernel(
    nmx, nmy,
    e_in, h_in, p_in, m_in, exit_ref,
    e_out, h_out, p_out, f_out,
    e, h, hp, eb, pq, mat, coef,
    xu, xd, yd, yu, xu_in, xd_in, yd_in, yu_in, gx, hs, es, ps,
    rmat, bw, tt, ff, cbuf, ra, own, other, gbuf, gall, fbuf,
    in_sem, out_sem, swap_send, swap_recv, back_send, back_recv, known,
    s_send, s_recv, p_send, p_recv, a_send, a_recv, b_send, b_recv,
):
    depth, cx, cy = mat.shape
    half = depth // 2
    mx, my, dz = lax.axis_index("mx"), lax.axis_index("my"), lax.axis_index("dz")
    partner = (mx, my, 1 - dz)
    up_m, down_m = lax.rem(mx + 1, nmx), lax.rem(mx + nmx - 1, nmx)
    up_y, down_y = lax.rem(my + 1, nmy), lax.rem(my + nmy - 1, nmy)
    right, left = lax.rem(mx + dz, nmx), lax.rem(mx + dz + nmx - 1, nmx)

    own_z, own_x = pl.ds(pl.multiple_of(half * dz, half), half), pl.ds(pl.multiple_of(cx * dz, cx), cx)
    far_z, far_x = pl.ds(pl.multiple_of(half - half * dz, half), half), pl.ds(pl.multiple_of(cx - cx * dz, cx), cx)
    blocks_in = (
        (m_in, mat, ()),
        (e_in, e, (slice(None),)),
        (h_in, h, (slice(None),)),
        (p_in, pq, (slice(None), slice(None))),
    )
    loads = [
        pltpu.make_async_copy(src.at[(*lead, slice(None), own_x)], dst.at[(*lead, own_z)], in_sem.at[i])
        for i, (src, dst, lead) in enumerate(blocks_in)
    ]
    for load in loads:
        load.start()

    barrier = pltpu.get_barrier_semaphore()
    peers = [(up_m, my, dz), (down_m, my, dz), (mx, up_y, dz), (mx, down_y, dz)]
    peers += [(at, to_y, 1 - dz) for at in (right, left) for to_y in (my, up_y, down_y)]
    for peer in peers:
        pl.semaphore_signal(barrier, inc=1, device_id=peer, device_id_type=MESH)

    one, zero = np.float32(1.0), np.float32(0.0)
    place_x = 2 * mx + dz
    xp, xm = jnp.where(place_x < 2 * nmx - 1, one, zero), jnp.where(place_x > 0, one, zero)
    yp, ym = jnp.where(my < nmy - 1, one, zero), jnp.where(my > 0, one, zero)

    lane = lax.broadcasted_iota(jnp.int32, (cx, cy), 1)
    row = lax.broadcasted_iota(jnp.int32, (cx, cy), 0)
    at_lane0, at_lane_end = lane == 0, lane == cy - 1
    at_row0, at_row_end = row == 0, row == cx - 1
    slab_lane = lax.broadcasted_iota(jnp.int32, (depth, cy), 1)
    slab_row = lax.broadcasted_iota(jnp.int32, (depth, cy), 0)
    slab_lane0, slab_lane_end = slab_lane == 0, slab_lane == cy - 1
    nothing = jnp.zeros((cx, cy), F32)
    slab_nothing = jnp.zeros((depth, cy), F32)

    def to(x, src, dst):
        shift = (dst - src) % cy
        return pltpu.roll(x, shift, axis=1) if shift else x

    def y_next(x):
        return pltpu.roll(x, cy - 1, axis=1)

    def y_last(x):
        return pltpu.roll(x, 1, axis=1)

    def x_next(x):
        return pltpu.roll(x, cx - 1, axis=0)

    def x_last(x):
        return pltpu.roll(x, 1, axis=0)

    def wide(x):
        return jnp.broadcast_to(x, (cx, cy))

    def slot(tile, which):
        return to(tile, which * depth, 0)

    def tile_up(x):
        lanes = lax.broadcasted_iota(jnp.int32, x.shape, 1)
        return jnp.where(lanes == depth - 1, zero, y_next(x)) - x

    def tile_down(x):
        lanes = lax.broadcasted_iota(jnp.int32, x.shape, 1)
        return x - jnp.where(lanes == 0, zero, y_last(x))

    def slab_up(x):
        return jnp.where(slab_row == depth - 1, zero, pltpu.roll(x, depth - 1, axis=0)) - x

    def slab_down(x):
        return x - jnp.where(slab_row == 0, zero, pltpu.roll(x, 1, axis=0))

    def column(x):
        picked = jnp.where(slab_lane == slab_row, jnp.broadcast_to(x, (depth, cy)), slab_nothing)
        return jnp.sum(picked, axis=1, keepdims=True)

    def at_end(x):
        return jnp.where(slab_lane_end, column(x), slab_nothing)

    def at_start(x):
        return jnp.where(slab_lane0, column(x), slab_nothing)

    def poles_of(z, fields):
        keep_d, drive_d, keep_l, drive_l, restore_l, scale = [coef[i, z] for i in range(6)]
        rest = []
        for c, field in enumerate(fields):
            polar, current, drude = pq[0, c, z], pq[1, c, z], pq[2, c, z]
            current_new = keep_l * current + drive_l * field - restore_l * polar
            drude_new = keep_d * drude + drive_d * field
            pq[0, c, z] = polar + DT * current_new
            pq[1, c, z] = current_new
            pq[2, c, z] = drude_new
            rest.append(field - scale * (0.5 * (drude + drude_new) + current_new))
        return rest, scale

    def begin_round(r):
        low_tile = high_tile = nothing
        hx_below = hy_below = nothing
        for z in range(depth):
            ex, ey, ez = e[0, z], e[1, z], e[2, z]
            exn, eyn = (e[0, z + 1], e[1, z + 1]) if z + 1 < depth else (nothing, nothing)
            dy_ez = jnp.where(at_lane_end, nothing, y_next(ez)) - ez
            dy_ex = jnp.where(at_lane_end, nothing, y_next(ex)) - ex
            dx_ez = jnp.where(at_row_end, nothing, x_next(ez)) - ez
            dx_ey = jnp.where(at_row_end, nothing, x_next(ey)) - ey
            hx = h[0, z] - DT * (dy_ez - (eyn - ey))
            hy = h[1, z] - DT * ((exn - ex) - dx_ez)
            hz = h[2, z] - DT * (dx_ey - dy_ex)
            hp[0, z], hp[1, z], hp[2, z] = hx, hy, hz
            rest, scale = poles_of(z, (ex, ey, ez))
            eb[0, z], eb[1, z], eb[2, z] = rest
            dx_hy = hy - jnp.where(at_row0, nothing, x_last(hy))
            dx_hz = hz - jnp.where(at_row0, nothing, x_last(hz))
            dy_hx = hx - jnp.where(at_lane0, nothing, y_last(hx))
            dy_hz = hz - jnp.where(at_lane0, nothing, y_last(hz))
            px = rest[0] + scale * (dy_hz - (hy - hy_below))
            py = rest[1] + scale * ((hx - hx_below) - dx_hz)
            pz = rest[2] + scale * (dx_hy - dy_hx)
            hx_below, hy_below = hx, hy
            for i, x in enumerate((hy, hz, px, py, pz, scale)):
                xu[r, i, z : z + 1, :] = x[cx - 1 : cx]
            for i, x in enumerate((ey, ez, py, pz, scale)):
                xd[r, i, z : z + 1, :] = x[0:1]
            for i, x in enumerate((ex, ez, px, pz, scale, ey, hy)):
                low_tile = jnp.where(lane == i * depth + z, to(x, 0, i * depth + z), low_tile)
            mixed = jnp.where(at_row0, ez, jnp.where(row == 1, x_last(y_last(ey)), hy))
            for i, x in enumerate((hx, hz, px, py, pz, scale, ey, mixed)):
                high_tile = jnp.where(lane == i * depth + z, to(x, cy - 1, i * depth + z), high_tile)
        yd[r] = low_tile
        yu[r] = high_tile

    def messages(r):
        there = 1 - dz
        table = (
            (yd.at[r], yd_in.at[r, 1], (right, down_y, there)),
            (yu.at[r], yu_in.at[r, 1], (left, up_y, there)),
            (yd.at[r], yd_in.at[r, 2], (left, down_y, there)),
            (yu.at[r], yu_in.at[r, 2], (right, up_y, there)),
            (xu.at[r], xu_in.at[r], (right, my, there)),
            (xd.at[r], xd_in.at[r], (left, my, there)),
            (yd.at[r], yd_in.at[r, 3], (right, my, there)),
            (yd.at[r], yd_in.at[r, 4], (left, my, there)),
            (yd.at[r], yd_in.at[r, 0], (mx, down_y, dz)),
            (yu.at[r], yu_in.at[r, 0], (mx, up_y, dz)),
        )
        return [
            pltpu.make_async_remote_copy(
                src_ref=src, dst_ref=dst, send_sem=s_send.at[r, k], recv_sem=s_recv.at[r, k],
                device_id=device, device_id_type=MESH,
            )
            for k, (src, dst, device) in enumerate(table)
        ]

    def electric_at(z, fields, below, hx_ym, hz_ym, rest, scale):
        hx, hy, hz = fields
        dx_hy = hy - jnp.where(at_row0, wide(gx[0, z : z + 1, :]), x_last(hy))
        dx_hz = hz - jnp.where(at_row0, wide(gx[1, z : z + 1, :]), x_last(hz))
        dy_hx = hx - jnp.where(at_lane0, to(hx_ym, z, 0), y_last(hx))
        dy_hz = hz - jnp.where(at_lane0, to(hz_ym, z, 0), y_last(hz))
        ex = rest[0] + scale * (dy_hz - (hy - below[1]))
        ey = rest[1] + scale * ((hx - below[0]) - dx_hz)
        ez = rest[2] + scale * (dx_hy - dy_hx)
        return ex, ey, ez

    def here_of(z):
        return jnp.where(exit_ref[0] == z, one, zero)

    def finish_round(r):
        own_low = yd[r]
        top = yd_in[r, 0] * yp
        left_top, right_top = yd_in[r, 1] * (xm * yp), yd_in[r, 2] * (xp * yp)
        left_low, right_low = yd_in[r, 3] * xm, yd_in[r, 4] * xp
        bottom = yu_in[r, 0] * ym
        right_bottom, left_bottom = yu_in[r, 1] * (xp * ym), yu_in[r, 2] * (xm * ym)
        end = cx - 1
        lt = left_top[end : end + 1]
        lt_ex, lt_ez, lt_px, lt_scale, lt_hy = [slot(lt, i) for i in (0, 1, 2, 4, 6)]
        lt_ex2 = left_top[end - 1 : end]
        rb = right_bottom[0:1]
        rb_hx, rb_py, rb_scale, rb_ey, rb_ez = [slot(rb, i) for i in (0, 3, 5, 6, 7)]
        rb_ey2 = slot(right_bottom[1:2], 7)
        lb = left_bottom[end : end + 1]
        lb_hx, lb_hz, lb_hy = [slot(lb, i) for i in (0, 1, 7)]
        rt = right_top[0:1]
        rt_ex, rt_ez, rt_ey = [slot(rt, i) for i in (0, 1, 5)]
        l_ex, l_ez = [slot(left_low[end : end + 1], i) for i in (0, 1)]
        r_ex, r_ez = [slot(right_low[0:1], i) for i in (0, 1)]
        t_ez, t_ey = [slot(top[0:1], i) for i in (1, 5)]
        b_ey, b_ez = slot(bottom[0:1], 6), slot(bottom[0:1], 7)

        corner_hx = (lb_hx - DT * l_ez) * (xm * ym)
        corner_hy = (lb_hy + DT * b_ez) * (xm * ym)
        corner_hz = (lb_hz - DT * b_ey + DT * l_ex) * (xm * ym)
        rb_hx = (rb_hx - DT * r_ez) * (xp * ym)
        lt_hy = (lt_hy + DT * t_ez) * (xm * yp)
        lt_ex_end = at_end(DT * lt_ex)
        more_hy_x = DT * xd[r, 1]
        more_hz_x = lt_ex_end - DT * xd[r, 0]
        hy_x = (xu_in[r, 0] + more_hy_x) * xm
        hz_x = (xu_in[r, 1] + more_hz_x) * xm
        more_hx_y = -DT * slot(own_low, 1)
        more_hz_y = DT * slot(own_low, 0) - jnp.where(at_row_end, DT * rb_ey, nothing)
        hx_y = (bottom + more_hx_y) * ym
        hz_y = (slot(bottom, 1) + more_hz_y) * ym
        gx[0], gx[1] = hy_x, hz_x

        plane = [nothing, nothing]
        below = (nothing, nothing)
        ex_low = ez_low = hx_high = hz_high = nothing
        for z in range(depth):
            hx, hy, hz = hp[0, z], hp[1, z], hp[2, z]
            hy = hy + jnp.where(at_row_end, wide(xd_in[r, 1, z : z + 1, :] * (DT * xp)), nothing)
            hz = hz - jnp.where(at_row_end, wide(xd_in[r, 0, z : z + 1, :] * (DT * xp)), nothing)
            hx = hx - jnp.where(at_lane_end, DT * to(top, depth + z, cy - 1), nothing)
            hz = hz + jnp.where(at_lane_end, DT * to(top, z, cy - 1), nothing)
            h[0, z], h[1, z], h[2, z] = hx, hy, hz
            fields = electric_at(z, (hx, hy, hz), below, hx_y, hz_y, (eb[0, z], eb[1, z], eb[2, z]), coef[5, z])
            below = (hx, hy)
            ex, ey, ez = fields
            e[0, z], e[1, z], e[2, z] = fields
            rest, _ = poles_of(z, fields)
            eb[0, z], eb[1, z], eb[2, z] = rest
            here = here_of(z)
            plane = [plane[0] + here * ex, plane[1] + here * ey]
            hs[0, z : z + 1, :] = hy[cx - 1 : cx]
            hs[1, z : z + 1, :] = hz[cx - 1 : cx]
            es[0, z : z + 1, :] = ey[0:1]
            es[1, z : z + 1, :] = ez[0:1]
            ex_low = jnp.where(lane == z, to(ex, 0, z), ex_low)
            ez_low = jnp.where(lane == z, to(ez, 0, z), ez_low)
            hx_high = jnp.where(lane == z, to(hx, cy - 1, z), hx_high)
            hz_high = jnp.where(lane == z, to(hz, cy - 1, z), hz_high)
        ps[2 * r, 0], ps[2 * r, 1] = plane

        more_hx = at_end(-DT * rt_ez)
        more_hz = at_end(DT * rt_ex)
        scale = xd_in[r, 4] * xp
        ey_right = xd_in[r, 2] * xp + scale * (slab_down(more_hx) - more_hz + hs[1])
        ez_right = xd_in[r, 3] * xp + scale * (at_start(rb_hx) - hs[0] - more_hx)
        gx_e = (ey_right, ez_right)

        more_hx = at_end(-DT * lt_ez)
        scale = xu_in[r, 5]
        hz_shift = jnp.where(slab_lane0, column(corner_hz), pltpu.roll(more_hz_x, 1, axis=1))
        ex_left = xu_in[r, 2] + scale * (more_hz_x - hz_shift - slab_down(more_hy_x))
        ey_left = xu_in[r, 3] + scale * (slab_down(more_hx) - (more_hz_x - at_end(DT * lt_ex2)))
        ez_left = xu_in[r, 4] + scale * (more_hy_x - more_hx + at_start(corner_hx))
        lt_more = column(-DT * t_ey - tile_down(DT * t_ez))
        ex_lt = column(lt_px) + column(lt_scale) * (lt_more - hz_x)

        more_hy = jnp.where(at_row_end, DT * rt_ez, nothing)
        more_hz = jnp.where(at_row_end, -DT * rt_ey, nothing)
        scale = slot(top, 4)
        ex_top = slot(top, 2) + scale * (more_hz - hz_high - tile_down(more_hy))
        ez_top = slot(top, 3) + scale * (more_hy - jnp.where(at_row0, lt_hy, nothing) + hx_high)

        more_hy = jnp.where(at_row_end, DT * rb_ez, nothing)
        scale = slot(bottom, 5)
        hz_two = jnp.where(at_row_end, -DT * rb_ey2, nothing)
        ex_bottom = slot(bottom, 2) + scale * (more_hz_y - hz_two - tile_down(more_hy))
        hz_shift = jnp.where(at_row0, wide(corner_hz), x_last(more_hz_y))
        ey_bottom = slot(bottom, 3) + scale * (tile_down(more_hx_y) - (more_hz_y - hz_shift))
        ez_bottom = slot(bottom, 4) + scale * (more_hy - jnp.where(at_row0, corner_hy, nothing) - more_hx_y)
        ey_rb = rb_py + rb_scale * (hz_y[end : end + 1] - DT * r_ex - tile_down(DT * r_ez))

        gx[0] = (hy_x - DT * (slab_up(ex_left) - (es[1] - ez_left))) * xm
        ex_next = jnp.where(slab_lane_end, ex_lt, pltpu.roll(ex_left, cy - 1, axis=1))
        gx[1] = (hz_x - DT * ((es[0] - ey_left) - (ex_next - ex_left))) * xm
        hx_y = (hx_y - DT * ((ez_low - ez_bottom) - tile_up(ey_bottom))) * ym
        ey_next = jnp.where(at_row_end, wide(ey_rb), x_next(ey_bottom))
        hz_y = (hz_y - DT * ((ey_next - ey_bottom) - (ex_low - ex_bottom))) * ym
        hs[0], hs[1] = gx_e

        plane = [nothing, nothing]
        below = (nothing, nothing)
        for z in range(depth):
            ex, ey, ez = e[0, z], e[1, z], e[2, z]
            exn, eyn = (e[0, z + 1], e[1, z + 1]) if z + 1 < depth else (nothing, nothing)
            dy_ez = jnp.where(at_lane_end, to(ez_top, z, cy - 1), y_next(ez)) - ez
            dy_ex = jnp.where(at_lane_end, to(ex_top, z, cy - 1), y_next(ex)) - ex
            dx_ez = jnp.where(at_row_end, wide(hs[1, z : z + 1, :]), x_next(ez)) - ez
            dx_ey = jnp.where(at_row_end, wide(hs[0, z : z + 1, :]), x_next(ey)) - ey
            hx = h[0, z] - DT * (dy_ez - (eyn - ey))
            hy = h[1, z] - DT * ((exn - ex) - dx_ez)
            hz = h[2, z] - DT * (dx_ey - dy_ex)
            h[0, z], h[1, z], h[2, z] = hx, hy, hz
            fields = electric_at(z, (hx, hy, hz), below, hx_y, hz_y, (eb[0, z], eb[1, z], eb[2, z]), coef[5, z])
            below = (hx, hy)
            e[0, z], e[1, z], e[2, z] = fields
            here = here_of(z)
            plane = [plane[0] + here * fields[0], plane[1] + here * fields[1]]
        ps[2 * r + 1, 0], ps[2 * r + 1, 1] = plane

    dzf, mxf, myf = dz.astype(F32), mx.astype(F32), my.astype(F32)
    vrow = lax.broadcasted_iota(jnp.int32, (V, cy), 0).astype(F32) - np.float32(V // 2)
    ypos = lax.broadcasted_iota(jnp.int32, (V, cy), 1).astype(F32) + (myf - np.float32(nmy // 2)) * np.float32(cy)
    size = np.float32(1.0 / math.sqrt(nmy * cy))
    for w in range(W):
        turn = fold(vrow * ypos, np.float32(V * (5 + w)), np.float32(1.0 / (V * (5 + w))))
        bw[w, :, 0:cy] = size * cos_turn(turn)
        bw[w, :, cy : 2 * cy] = -size * sin_turn(turn)

    r = lax.broadcasted_iota(jnp.int32, (128, 128), 0)
    c = lax.broadcasted_iota(jnp.int32, (128, 128), 1)
    w_r, w_c = (r // 32) % 2, (c // 32) % 2
    own_u = (r % 8).astype(F32) + (mxf * np.float32(8) - np.float32(U // 2))
    inverse = jnp.where(
        w_r == 0,
        jnp.where(dz == 0, np.float32(1.0 / (U * 5)), np.float32(1.0 / (U * 7))),
        jnp.where(dz == 0, np.float32(1.0 / (U * 6)), np.float32(1.0 / (U * 8))),
    )
    quarter = ((r // 16) % 2 - (c // 16) % 2 - r // 64).astype(F32) * np.float32(0.25)
    turn = own_u * (c % 8 + 8 * (c // 64)).astype(F32) * inverse + quarter
    turn = turn - jnp.floor(turn + 0.5)
    same = (w_r == w_c) & ((r // 8) % 2 == (c // 8) % 2)
    tt[...] = jnp.where(same, np.float32(1.0 / math.sqrt(nmx * 2 * cx)) * cos_turn(turn), zero)

    width = 8 * nmx
    r = lax.broadcasted_iota(jnp.int32, (64, width), 0)
    c = lax.broadcasted_iota(jnp.int32, (64, width), 1)
    own_u = (r % 8).astype(F32) + (mxf * np.float32(8) - np.float32(U // 2))
    parts = U // (2 * cx)
    q = (5 + r // 32).astype(F32) + 2 * dzf
    inverse = jnp.where(
        r // 32 == 0,
        jnp.where(dz == 0, np.float32(1.0 / (parts * 5)), np.float32(1.0 / (parts * 7))),
        jnp.where(dz == 0, np.float32(1.0 / (parts * 6)), np.float32(1.0 / (parts * 8))),
    )
    turn = fold(own_u * ((c // 8).astype(F32) - np.float32(nmx // 2)), q * np.float32(parts), inverse)
    ff[0] = cos_turn(turn)
    ff[1] = -sin_turn(turn)

    for load in loads:
        load.wait()
    pl.semaphore_wait(barrier, len(peers))

    def remote(src, dst, send, recv, device):
        return pltpu.make_async_remote_copy(
            src_ref=src, dst_ref=dst, send_sem=send, recv_sem=recv, device_id=device, device_id_type=MESH
        )

    swaps = [
        remote(
            src.at[(*lead, slice(None), far_x)], dst.at[(*lead, own_z)], swap_send.at[i], swap_recv.at[i], partner
        )
        for i, (src, dst, lead) in enumerate(blocks_in)
    ]
    for swap in swaps:
        swap.start()

    def spread(i):
        for far in (1 << i, -(1 << i)):
            to_x, to_y = lax.rem(mx + far + 2 * nmx, nmx), lax.rem(my + far + 2 * nmy, nmy)
            pl.semaphore_signal(known.at[0, i], inc=1, device_id=(to_x, my, dz), device_id_type=MESH)
            pl.semaphore_signal(known.at[1, i], inc=1, device_id=(mx, to_y, dz), device_id_type=MESH)

    def heard(i):
        pl.semaphore_wait(known.at[0, i], 2)
        pl.semaphore_wait(known.at[1, i], 2)

    spread(0)
    swaps[0].wait()
    for z in range(depth):
        kind = mat[z]
        for i in range(6):
            t = coef_table[i]
            coef[i, z] = jnp.where(kind < 2, jnp.where(kind == 0, t[0], t[1]), jnp.where(kind == 2, t[2], t[3]))
    for swap in swaps[1:]:
        swap.wait()

    def two_steps(r, carry):
        begin_round(r)
        sent = messages(r)
        for m in sent:
            m.start()
        for m in sent:
            m.wait()

        @pl.when(r == 0)
        def _():
            heard(0)
            spread(1)

        @pl.when(r == 1)
        def _():
            heard(1)
            spread(2)

        finish_round(r)
        return carry

    lax.fori_loop(0, STEPS // 2, two_steps, 0)

    blocks_out = (
        (e, e_out, (slice(None),)),
        (h, h_out, (slice(None),)),
        (pq, p_out, (slice(None), slice(None))),
    )
    stores = [
        pltpu.make_async_copy(src.at[(*lead, own_z)], dst.at[(*lead, slice(None), own_x)], out_sem.at[i])
        for i, (src, dst, lead) in enumerate(blocks_out)
    ]
    stores += [
        remote(
            src.at[(*lead, far_z)], dst.at[(*lead, slice(None), own_x)], back_send.at[i], back_recv.at[i], partner
        )
        for i, (src, dst, lead) in enumerate(blocks_out)
    ]

    columns = []
    for w in range(W):
        parts_of = []
        for p in range(2):
            re = im = nothing
            for s in range(STEPS):
                angle = 2 * math.pi * (s + 1) / (8 + 2 * w)
                re = re + np.float32(math.cos(angle)) * ps[s, p]
                im = im - np.float32(math.sin(angle)) * ps[s, p]
            parts_of.append((re, im))
        re = jnp.concatenate([parts_of[0][0], parts_of[1][0]], 0)
        im = jnp.concatenate([parts_of[0][1], parts_of[1][1]], 0)
        rmat[w, 0 : 2 * cx, 0:cy] = re
        rmat[w, 0 : 2 * cx, cy : 2 * cy] = -im
        rmat[w, 2 * cx : 4 * cx, 0:cy] = im
        rmat[w, 2 * cx : 4 * cx, cy : 2 * cy] = re
        columns.append(
            lax.dot_general(
                bw[w], rmat[w], (((1,), (1,)), ((), ())),
                precision=lax.Precision.HIGHEST, preferred_element_type=F32,
            )
        )
    cbuf[...] = jnp.concatenate(columns, 1).reshape(nmy, 8, 128)

    heard(2)
    sent = []
    for k in range(1, nmy):
        to_y = lax.rem(my + k, nmy)
        m = remote(cbuf.at[to_y], ra.at[k], a_send.at[k], a_recv.at[k], (mx, to_y, dz))
        m.start()
        sent.append(m)
    for store in stores:
        store.start()
    total = cbuf[my]
    for k, m in enumerate(sent):
        m.wait()
        total = total + ra[k + 1]
    own[...] = total
    pair = remote(own, other, p_send.at[0], p_recv.at[0], partner)
    pair.start()
    pair.wait()
    mine = lax.broadcasted_iota(jnp.int32, (8, 128), 1) // 64 == dz
    total = jnp.where(mine, total, pltpu.roll(other[...], 64, axis=1))
    gbuf[...] = total
    gall[mx] = total
    sent = []
    for k in range(1, nmx):
        m = remote(gbuf, gall.at[mx], b_send.at[k], b_recv.at[k], (lax.rem(mx + k, nmx), my, dz))
        m.start()
        sent.append(m)
    for m in sent:
        m.wait()
    both = lax.dot_general(
        tt[...], gall[...].reshape(width, 128), (((1,), (1,)), ((), ())),
        precision=lax.Precision.HIGHEST, preferred_element_type=F32,
    )
    far = both[0:64] * ff[0] + both[64:128] * ff[1]
    shift = 8
    while shift < width:
        far = far + pltpu.roll(far, shift, axis=1)
        shift *= 2
    far = far.reshape(2, 2, 2, 8, width)
    fbuf[...] = far[..., 0:8]
    last = pltpu.make_async_copy(fbuf, f_out, out_sem.at[3])
    last.start()
    for store in stores:
        store.wait()
    last.wait()


def hand_over(*refs):
    ins, outs, held, sems = refs[:4], refs[4:8], refs[8:12], refs[12]
    first = [pltpu.make_async_copy(a, b, sems.at[0, i]) for i, (a, b) in enumerate(zip(ins, held))]
    then = [pltpu.make_async_copy(a, b, sems.at[1, i]) for i, (a, b) in enumerate(zip(held, outs))]
    for copy in first:
        copy.start()
    for copy, after in zip(first, then):
        copy.wait()
        after.start()
    for after in then:
        after.wait()


def body(nmx, nmy, electric, magnetic, poles, material, exit_layer):
    near, cx, cy = material.shape
    depth, mine = 2 * near, cx // 2
    vm = lambda *shape: pltpu.VMEM(shape, F32)
    dma = lambda *shape: pltpu.SemaphoreType.DMA(shape)
    anywhere = pl.BlockSpec(memory_space=pl.ANY)
    field = (3, near, cx, cy)
    held = (3, depth, mine, cy)
    share = (2, 2, 2, U // nmx, V // nmy)
    n = STEPS // 2
    outs = pl.pallas_call(
        functools.partial(kernel, nmx, nmy),
        out_shape=(
            jax.ShapeDtypeStruct(field, F32),
            jax.ShapeDtypeStruct(field, F32),
            jax.ShapeDtypeStruct((3, *field), F32),
            jax.ShapeDtypeStruct(share, F32),
        ),
        in_specs=[anywhere] * 4 + [pl.BlockSpec(memory_space=pltpu.SMEM)],
        out_specs=[anywhere] * 4,
        scratch_shapes=[
            vm(*held), vm(*held), vm(*held), vm(*held), vm(3, *held),
            pltpu.VMEM((depth, mine, cy), jnp.int32), vm(6, depth, mine, cy),
            vm(n, 6, depth, cy), vm(n, 5, depth, cy), vm(n, mine, cy), vm(n, mine, cy),
            vm(n, 6, depth, cy), vm(n, 5, depth, cy), vm(n, 5, mine, cy), vm(n, 3, mine, cy),
            vm(2, depth, cy), vm(2, depth, cy), vm(2, depth, cy), vm(STEPS, 2, mine, cy),
            vm(W, 4 * mine, 2 * cy), vm(W, V, 2 * cy), vm(128, 128), vm(2, 64, 8 * nmx),
            vm(nmy, 8, 128), vm(nmy, 8, 128), vm(8, 128), vm(8, 128), vm(8, 128), vm(nmx, 8, 128), vm(*share),
            dma(4), dma(4), dma(4), dma(4), dma(3), dma(3), pltpu.SemaphoreType.REGULAR((2, 3)),
            dma(n, 10), dma(n, 10), dma(1), dma(1), dma(nmy), dma(nmy), dma(nmx), dma(nmx),
        ],
        compiler_params=pltpu.CompilerParams(collective_id=0, has_side_effects=True),
    )(electric, magnetic, poles, material, exit_layer)
    shapes = (field, field, (3, *field), share)
    return pl.pallas_call(
        hand_over,
        out_shape=tuple(jax.ShapeDtypeStruct(shape, F32) for shape in shapes),
        in_specs=[anywhere] * 4,
        out_specs=[anywhere] * 4,
        scratch_shapes=[vm(*shape) for shape in shapes] + [dma(2, 4)],
    )(*outs)


def solution(mesh):
    nmx, nmy = mesh.shape["mx"], mesh.shape["my"]
    return jax.shard_map(
        functools.partial(body, nmx, nmy),
        mesh=mesh,
        in_specs=(
            P(None, "dz", "mx", "my"),
            P(None, "dz", "mx", "my"),
            P(None, None, "dz", "mx", "my"),
            P("dz", "mx", "my"),
            P(),
        ),
        out_specs=(
            P(None, "dz", "mx", "my"),
            P(None, "dz", "mx", "my"),
            P(None, None, "dz", "mx", "my"),
            P("dz", None, None, "mx", "my"),
        ),
        check_vma=False,
    )
```

```python
import functools
import math

import jax
import jax.numpy as jnp
import numpy as np
from jax import lax
from jax.experimental import pallas as pl
from jax.experimental.pallas import tpu as pltpu
from jax.sharding import PartitionSpec as P

STEPS = 4
W = 4
U = 128
V = 128
MESH = pl.DeviceIdType.MESH
F32 = jnp.float32

time_step = 0.5
eps_inf = np.array([1.0, 4.0, 2.1, 1.5])
drude_plasma = np.array([0.0, 0.0, 0.0, 2.0])
drude_damping = np.array([0.0, 0.0, 0.0, 0.1])
lorentz_square = np.array([0.3, 0.8, 1.0, 0.5])
lorentz_strength = np.array([0.0, 1.5, 0.1, 0.8])
lorentz_damping = np.array([0.0, 0.05, 0.02, 0.2])
drude_keep = (1.0 - drude_damping * time_step / 2) / (1.0 + drude_damping * time_step / 2)
drude_drive = drude_plasma * time_step / (1.0 + drude_damping * time_step / 2)
lorentz_keep = (1.0 - lorentz_damping * time_step / 2) / (1.0 + lorentz_damping * time_step / 2)
lorentz_push = time_step / (1.0 + lorentz_damping * time_step / 2)
coef_table = np.stack(
    [
        drude_keep,
        drude_drive,
        lorentz_keep,
        lorentz_push * lorentz_square * lorentz_strength,
        lorentz_push * lorentz_square,
        time_step / eps_inf,
    ]
).astype(np.float32)
DT = np.float32(time_step)

COS_TERMS = [np.float32((-1) ** k * (2 * math.pi) ** (2 * k) / math.factorial(2 * k)) for k in range(11)]
SIN_TERMS = [np.float32((-1) ** k * (2 * math.pi) ** (2 * k + 1) / math.factorial(2 * k + 1)) for k in range(11)]


GROUP = 8


def poly(terms, z):
    value = jnp.full_like(z, terms[-1])
    for term in terms[-2::-1]:
        value = value * z + term
    return value


def cos_turn(t):
    return poly(COS_TERMS, t * t)


def sin_turn(t):
    return t * poly(SIN_TERMS, t * t)


def in_two(x):
    high = x.astype(jnp.bfloat16)
    return high, (x - high.astype(F32)).astype(jnp.bfloat16)


def matmul(a, b):
    return lax.dot_general(a, b, (((1,), (1,)), ((), ())), preferred_element_type=F32)


def fold(product, period, inverse):
    left = product - jnp.floor(product * inverse + 0.5) * period
    return left * inverse


def kernel(
    nmx, nmy,
    e_in, h_in, p_in, m_in, exit_ref,
    e_out, h_out, p_out, f_out,
    e, h, hp, eb, pq, mat, coef,
    xu, xd, yd, yu, xu_in, xd_in, yd_in, yu_in, gx, hs, es, ps,
    ct, bw_high, bw_low, tt, ff, cbuf, ra, own, other, gbuf, gall, fbuf,
    in_sem, out_sem, swap_send, swap_recv, back_send, back_recv, known,
    s_send, s_recv, p_send, p_recv, a_send, a_recv, b_send, b_recv,
):
    depth, cx, cy = mat.shape
    half = depth // 2
    mx, my, dz = lax.axis_index("mx"), lax.axis_index("my"), lax.axis_index("dz")
    partner = (mx, my, 1 - dz)
    up_m, down_m = lax.rem(mx + 1, nmx), lax.rem(mx + nmx - 1, nmx)
    up_y, down_y = lax.rem(my + 1, nmy), lax.rem(my + nmy - 1, nmy)
    right, left = lax.rem(mx + dz, nmx), lax.rem(mx + dz + nmx - 1, nmx)

    own_z, own_x = pl.ds(pl.multiple_of(half * dz, half), half), pl.ds(pl.multiple_of(cx * dz, cx), cx)
    far_z, far_x = pl.ds(pl.multiple_of(half - half * dz, half), half), pl.ds(pl.multiple_of(cx - cx * dz, cx), cx)
    blocks_in = (
        (m_in, mat, ()),
        (e_in, e, (slice(None),)),
        (h_in, h, (slice(None),)),
        (p_in, pq, (slice(None), slice(None))),
    )
    loads = [
        pltpu.make_async_copy(src.at[(*lead, slice(None), own_x)], dst.at[(*lead, own_z)], in_sem.at[i])
        for i, (src, dst, lead) in enumerate(blocks_in)
    ]
    for load in loads:
        load.start()

    barrier = pltpu.get_barrier_semaphore()
    peers = [(up_m, my, dz), (down_m, my, dz), (mx, up_y, dz), (mx, down_y, dz)]
    peers += [(at, to_y, 1 - dz) for at in (right, left) for to_y in (my, up_y, down_y)]
    for peer in peers:
        pl.semaphore_signal(barrier, inc=1, device_id=peer, device_id_type=MESH)

    one, zero = np.float32(1.0), np.float32(0.0)
    place_x = 2 * mx + dz
    xp, xm = jnp.where(place_x < 2 * nmx - 1, one, zero), jnp.where(place_x > 0, one, zero)
    yp, ym = jnp.where(my < nmy - 1, one, zero), jnp.where(my > 0, one, zero)

    lane = lax.broadcasted_iota(jnp.int32, (cx, cy), 1)
    row = lax.broadcasted_iota(jnp.int32, (cx, cy), 0)
    at_lane0, at_lane_end = lane == 0, lane == cy - 1
    at_row0, at_row_end = row == 0, row == cx - 1
    slab_lane = lax.broadcasted_iota(jnp.int32, (depth, cy), 1)
    slab_row = lax.broadcasted_iota(jnp.int32, (depth, cy), 0)
    slab_lane0, slab_lane_end = slab_lane == 0, slab_lane == cy - 1
    nothing = jnp.zeros((cx, cy), F32)
    slab_nothing = jnp.zeros((depth, cy), F32)

    def to(x, src, dst):
        shift = (dst - src + cy) % cy
        return pltpu.roll(x, shift, axis=1) if not isinstance(shift, int) or shift else x

    def layers(body, carry):
        def some(g, carry):
            for j in range(GROUP):
                carry = body(GROUP * g + j, carry)
            return carry

        return lax.fori_loop(0, depth // GROUP, some, carry)

    def y_next(x):
        return pltpu.roll(x, cy - 1, axis=1)

    def y_last(x):
        return pltpu.roll(x, 1, axis=1)

    def x_next(x):
        return pltpu.roll(x, cx - 1, axis=0)

    def x_last(x):
        return pltpu.roll(x, 1, axis=0)

    def wide(x):
        return jnp.broadcast_to(x, (cx, cy))

    def slot(tile, which):
        return to(tile, which * depth, 0)

    def tile_up(x):
        lanes = lax.broadcasted_iota(jnp.int32, x.shape, 1)
        return jnp.where(lanes == depth - 1, zero, y_next(x)) - x

    def tile_down(x):
        lanes = lax.broadcasted_iota(jnp.int32, x.shape, 1)
        return x - jnp.where(lanes == 0, zero, y_last(x))

    def slab_up(x):
        return jnp.where(slab_row == depth - 1, zero, pltpu.roll(x, depth - 1, axis=0)) - x

    def slab_down(x):
        return x - jnp.where(slab_row == 0, zero, pltpu.roll(x, 1, axis=0))

    def column(x):
        picked = jnp.where(slab_lane == slab_row, jnp.broadcast_to(x, (depth, cy)), slab_nothing)
        return jnp.sum(picked, axis=1, keepdims=True)

    def at_end(x):
        return jnp.where(slab_lane_end, column(x), slab_nothing)

    def at_start(x):
        return jnp.where(slab_lane0, column(x), slab_nothing)

    def poles_of(z, fields):
        keep_d, drive_d, keep_l, drive_l, restore_l, scale = [coef[i, z] for i in range(6)]
        rest = []
        for c, field in enumerate(fields):
            polar, current, drude = pq[0, c, z], pq[1, c, z], pq[2, c, z]
            current_new = keep_l * current + drive_l * field - restore_l * polar
            drude_new = keep_d * drude + drive_d * field
            pq[0, c, z] = polar + DT * current_new
            pq[1, c, z] = current_new
            pq[2, c, z] = drude_new
            rest.append(field - scale * (0.5 * (drude + drude_new) + current_new))
        return rest, scale

    def begin_round(r):
        def layer(z, carry):
            low_tile, high_tile, hx_below, hy_below = carry
            ex, ey, ez = e[0, z], e[1, z], e[2, z]
            exn, eyn = e[0, z + 1], e[1, z + 1]
            dy_ez = jnp.where(at_lane_end, nothing, y_next(ez)) - ez
            dy_ex = jnp.where(at_lane_end, nothing, y_next(ex)) - ex
            dx_ez = jnp.where(at_row_end, nothing, x_next(ez)) - ez
            dx_ey = jnp.where(at_row_end, nothing, x_next(ey)) - ey
            hx = h[0, z] - DT * (dy_ez - (eyn - ey))
            hy = h[1, z] - DT * ((exn - ex) - dx_ez)
            hz = h[2, z] - DT * (dx_ey - dy_ex)
            hp[0, z], hp[1, z], hp[2, z] = hx, hy, hz
            rest, scale = poles_of(z, (ex, ey, ez))
            eb[0, z], eb[1, z], eb[2, z] = rest
            dx_hy = hy - jnp.where(at_row0, nothing, x_last(hy))
            dx_hz = hz - jnp.where(at_row0, nothing, x_last(hz))
            dy_hx = hx - jnp.where(at_lane0, nothing, y_last(hx))
            dy_hz = hz - jnp.where(at_lane0, nothing, y_last(hz))
            px = rest[0] + scale * (dy_hz - (hy - hy_below))
            py = rest[1] + scale * ((hx - hx_below) - dx_hz)
            pz = rest[2] + scale * (dx_hy - dy_hx)
            for i, x in enumerate((hy, hz, px, py, pz, scale)):
                xu[r, i, pl.ds(z, 1), :] = x[cx - 1 : cx]
            for i, x in enumerate((ey, ez, py, pz, scale)):
                xd[r, i, pl.ds(z, 1), :] = x[0:1]
            for i, x in enumerate((ex, ez, px, pz, scale, ey, hy)):
                low_tile = jnp.where(lane == i * depth + z, to(x, 0, i * depth + z), low_tile)
            mixed = jnp.where(at_row0, ez, jnp.where(row == 1, x_last(y_last(ey)), hy))
            for i, x in enumerate((hx, hz, px, py, pz, scale, ey, mixed)):
                high_tile = jnp.where(lane == i * depth + z, to(x, cy - 1, i * depth + z), high_tile)
            return low_tile, high_tile, hx, hy

        low_tile, high_tile, _, _ = layers(layer, (nothing,) * 4)
        yd[r] = low_tile
        yu[r] = high_tile

    def messages(r):
        there = 1 - dz
        table = (
            (yd.at[r], yd_in.at[r, 1], (right, down_y, there)),
            (yu.at[r], yu_in.at[r, 1], (left, up_y, there)),
            (yd.at[r], yd_in.at[r, 2], (left, down_y, there)),
            (yu.at[r], yu_in.at[r, 2], (right, up_y, there)),
            (xu.at[r], xu_in.at[r], (right, my, there)),
            (xd.at[r], xd_in.at[r], (left, my, there)),
            (yd.at[r], yd_in.at[r, 3], (right, my, there)),
            (yd.at[r], yd_in.at[r, 4], (left, my, there)),
            (yd.at[r], yd_in.at[r, 0], (mx, down_y, dz)),
            (yu.at[r], yu_in.at[r, 0], (mx, up_y, dz)),
        )
        return [
            pltpu.make_async_remote_copy(
                src_ref=src, dst_ref=dst, send_sem=s_send.at[r, k], recv_sem=s_recv.at[r, k],
                device_id=device, device_id_type=MESH,
            )
            for k, (src, dst, device) in enumerate(table)
        ]

    def electric_at(z, fields, below, hx_ym, hz_ym, rest, scale):
        hx, hy, hz = fields
        dx_hy = hy - jnp.where(at_row0, wide(gx[0, pl.ds(z, 1), :]), x_last(hy))
        dx_hz = hz - jnp.where(at_row0, wide(gx[1, pl.ds(z, 1), :]), x_last(hz))
        dy_hx = hx - jnp.where(at_lane0, to(hx_ym, z, 0), y_last(hx))
        dy_hz = hz - jnp.where(at_lane0, to(hz_ym, z, 0), y_last(hz))
        ex = rest[0] + scale * (dy_hz - (hy - below[1]))
        ey = rest[1] + scale * ((hx - below[0]) - dx_hz)
        ez = rest[2] + scale * (dx_hy - dy_hx)
        return ex, ey, ez

    def here_of(z):
        return jnp.where(exit_ref[0] == z, one, zero)

    def finish_round(r):
        own_low = yd[r]
        top = yd_in[r, 0] * yp
        left_top, right_top = yd_in[r, 1] * (xm * yp), yd_in[r, 2] * (xp * yp)
        left_low, right_low = yd_in[r, 3] * xm, yd_in[r, 4] * xp
        bottom = yu_in[r, 0] * ym
        right_bottom, left_bottom = yu_in[r, 1] * (xp * ym), yu_in[r, 2] * (xm * ym)
        end = cx - 1
        lt = left_top[end : end + 1]
        lt_ex, lt_ez, lt_px, lt_scale, lt_hy = [slot(lt, i) for i in (0, 1, 2, 4, 6)]
        lt_ex2 = left_top[end - 1 : end]
        rb = right_bottom[0:1]
        rb_hx, rb_py, rb_scale, rb_ey, rb_ez = [slot(rb, i) for i in (0, 3, 5, 6, 7)]
        rb_ey2 = slot(right_bottom[1:2], 7)
        lb = left_bottom[end : end + 1]
        lb_hx, lb_hz, lb_hy = [slot(lb, i) for i in (0, 1, 7)]
        rt = right_top[0:1]
        rt_ex, rt_ez, rt_ey = [slot(rt, i) for i in (0, 1, 5)]
        l_ex, l_ez = [slot(left_low[end : end + 1], i) for i in (0, 1)]
        r_ex, r_ez = [slot(right_low[0:1], i) for i in (0, 1)]
        t_ez, t_ey = [slot(top[0:1], i) for i in (1, 5)]
        b_ey, b_ez = slot(bottom[0:1], 6), slot(bottom[0:1], 7)

        corner_hx = (lb_hx - DT * l_ez) * (xm * ym)
        corner_hy = (lb_hy + DT * b_ez) * (xm * ym)
        corner_hz = (lb_hz - DT * b_ey + DT * l_ex) * (xm * ym)
        rb_hx = (rb_hx - DT * r_ez) * (xp * ym)
        lt_hy = (lt_hy + DT * t_ez) * (xm * yp)
        lt_ex_end = at_end(DT * lt_ex)
        more_hy_x = DT * xd[r, 1]
        more_hz_x = lt_ex_end - DT * xd[r, 0]
        hy_x = (xu_in[r, 0] + more_hy_x) * xm
        hz_x = (xu_in[r, 1] + more_hz_x) * xm
        more_hx_y = -DT * slot(own_low, 1)
        more_hz_y = DT * slot(own_low, 0) - jnp.where(at_row_end, DT * rb_ey, nothing)
        hx_y = (bottom + more_hx_y) * ym
        hz_y = (slot(bottom, 1) + more_hz_y) * ym
        gx[0], gx[1] = hy_x, hz_x

        def first(z, carry):
            below, plane, ex_low, ez_low, hx_high, hz_high = carry
            hx, hy, hz = hp[0, z], hp[1, z], hp[2, z]
            hy = hy + jnp.where(at_row_end, wide(xd_in[r, 1, pl.ds(z, 1), :] * (DT * xp)), nothing)
            hz = hz - jnp.where(at_row_end, wide(xd_in[r, 0, pl.ds(z, 1), :] * (DT * xp)), nothing)
            hx = hx - jnp.where(at_lane_end, DT * to(top, depth + z, cy - 1), nothing)
            hz = hz + jnp.where(at_lane_end, DT * to(top, z, cy - 1), nothing)
            h[0, z], h[1, z], h[2, z] = hx, hy, hz
            fields = electric_at(z, (hx, hy, hz), below, hx_y, hz_y, (eb[0, z], eb[1, z], eb[2, z]), coef[5, z])
            ex, ey, ez = fields
            e[0, z], e[1, z], e[2, z] = fields
            rest, _ = poles_of(z, fields)
            eb[0, z], eb[1, z], eb[2, z] = rest
            here = here_of(z)
            plane = (plane[0] + here * ex, plane[1] + here * ey)
            hs[0, pl.ds(z, 1), :] = hy[cx - 1 : cx]
            hs[1, pl.ds(z, 1), :] = hz[cx - 1 : cx]
            es[0, pl.ds(z, 1), :] = ey[0:1]
            es[1, pl.ds(z, 1), :] = ez[0:1]
            ex_low = jnp.where(lane == z, to(ex, 0, z), ex_low)
            ez_low = jnp.where(lane == z, to(ez, 0, z), ez_low)
            hx_high = jnp.where(lane == z, to(hx, cy - 1, z), hx_high)
            hz_high = jnp.where(lane == z, to(hz, cy - 1, z), hz_high)
            return (hx, hy), plane, ex_low, ez_low, hx_high, hz_high

        pair = (nothing, nothing)
        _, plane, ex_low, ez_low, hx_high, hz_high = layers(first, (pair, pair, *pair, *pair))
        ps[2 * r, 0], ps[2 * r, 1] = plane

        more_hx = at_end(-DT * rt_ez)
        more_hz = at_end(DT * rt_ex)
        scale = xd_in[r, 4] * xp
        ey_right = xd_in[r, 2] * xp + scale * (slab_down(more_hx) - more_hz + hs[1])
        ez_right = xd_in[r, 3] * xp + scale * (at_start(rb_hx) - hs[0] - more_hx)
        gx_e = (ey_right, ez_right)

        more_hx = at_end(-DT * lt_ez)
        scale = xu_in[r, 5]
        hz_shift = jnp.where(slab_lane0, column(corner_hz), pltpu.roll(more_hz_x, 1, axis=1))
        ex_left = xu_in[r, 2] + scale * (more_hz_x - hz_shift - slab_down(more_hy_x))
        ey_left = xu_in[r, 3] + scale * (slab_down(more_hx) - (more_hz_x - at_end(DT * lt_ex2)))
        ez_left = xu_in[r, 4] + scale * (more_hy_x - more_hx + at_start(corner_hx))
        lt_more = column(-DT * t_ey - tile_down(DT * t_ez))
        ex_lt = column(lt_px) + column(lt_scale) * (lt_more - hz_x)

        more_hy = jnp.where(at_row_end, DT * rt_ez, nothing)
        more_hz = jnp.where(at_row_end, -DT * rt_ey, nothing)
        scale = slot(top, 4)
        ex_top = slot(top, 2) + scale * (more_hz - hz_high - tile_down(more_hy))
        ez_top = slot(top, 3) + scale * (more_hy - jnp.where(at_row0, lt_hy, nothing) + hx_high)

        more_hy = jnp.where(at_row_end, DT * rb_ez, nothing)
        scale = slot(bottom, 5)
        hz_two = jnp.where(at_row_end, -DT * rb_ey2, nothing)
        ex_bottom = slot(bottom, 2) + scale * (more_hz_y - hz_two - tile_down(more_hy))
        hz_shift = jnp.where(at_row0, wide(corner_hz), x_last(more_hz_y))
        ey_bottom = slot(bottom, 3) + scale * (tile_down(more_hx_y) - (more_hz_y - hz_shift))
        ez_bottom = slot(bottom, 4) + scale * (more_hy - jnp.where(at_row0, corner_hy, nothing) - more_hx_y)
        ey_rb = rb_py + rb_scale * (hz_y[end : end + 1] - DT * r_ex - tile_down(DT * r_ez))

        gx[0] = (hy_x - DT * (slab_up(ex_left) - (es[1] - ez_left))) * xm
        ex_next = jnp.where(slab_lane_end, ex_lt, pltpu.roll(ex_left, cy - 1, axis=1))
        gx[1] = (hz_x - DT * ((es[0] - ey_left) - (ex_next - ex_left))) * xm
        hx_y = (hx_y - DT * ((ez_low - ez_bottom) - tile_up(ey_bottom))) * ym
        ey_next = jnp.where(at_row_end, wide(ey_rb), x_next(ey_bottom))
        hz_y = (hz_y - DT * ((ey_next - ey_bottom) - (ex_low - ex_bottom))) * ym
        hs[0], hs[1] = gx_e

        def second(z, carry):
            below, plane = carry
            ex, ey, ez = e[0, z], e[1, z], e[2, z]
            exn, eyn = e[0, z + 1], e[1, z + 1]
            dy_ez = jnp.where(at_lane_end, to(ez_top, z, cy - 1), y_next(ez)) - ez
            dy_ex = jnp.where(at_lane_end, to(ex_top, z, cy - 1), y_next(ex)) - ex
            dx_ez = jnp.where(at_row_end, wide(hs[1, pl.ds(z, 1), :]), x_next(ez)) - ez
            dx_ey = jnp.where(at_row_end, wide(hs[0, pl.ds(z, 1), :]), x_next(ey)) - ey
            hx = h[0, z] - DT * (dy_ez - (eyn - ey))
            hy = h[1, z] - DT * ((exn - ex) - dx_ez)
            hz = h[2, z] - DT * (dx_ey - dy_ex)
            h[0, z], h[1, z], h[2, z] = hx, hy, hz
            fields = electric_at(z, (hx, hy, hz), below, hx_y, hz_y, (eb[0, z], eb[1, z], eb[2, z]), coef[5, z])
            e[0, z], e[1, z], e[2, z] = fields
            here = here_of(z)
            return (hx, hy), (plane[0] + here * fields[0], plane[1] + here * fields[1])

        _, plane = layers(second, (pair, pair))
        ps[2 * r + 1, 0], ps[2 * r + 1, 1] = plane

    for i in range(3):
        e[i, depth] = nothing

    dzf, mxf, myf = dz.astype(F32), mx.astype(F32), my.astype(F32)
    vrow = lax.broadcasted_iota(jnp.int32, (V, cy), 0).astype(F32) - np.float32(V // 2)
    ypos = lax.broadcasted_iota(jnp.int32, (V, cy), 1).astype(F32) + (myf - np.float32(nmy // 2)) * np.float32(cy)
    size = np.float32(1.0 / math.sqrt(nmy * cy))
    for w in range(W):
        turn = fold(vrow * ypos, np.float32(V * (5 + w)), np.float32(1.0 / (V * (5 + w))))
        bw_high[w, :, 0:cy], bw_low[w, :, 0:cy] = in_two(size * cos_turn(turn))
        bw_high[w, :, cy : 2 * cy], bw_low[w, :, cy : 2 * cy] = in_two(-size * sin_turn(turn))

    r = lax.broadcasted_iota(jnp.int32, (128, 128), 0)
    c = lax.broadcasted_iota(jnp.int32, (128, 128), 1)
    w_r, w_c = (r // 32) % 2, (c // 32) % 2
    own_u = (r % 8).astype(F32) + (mxf * np.float32(8) - np.float32(U // 2))
    inverse = jnp.where(
        w_r == 0,
        jnp.where(dz == 0, np.float32(1.0 / (U * 5)), np.float32(1.0 / (U * 7))),
        jnp.where(dz == 0, np.float32(1.0 / (U * 6)), np.float32(1.0 / (U * 8))),
    )
    quarter = ((r // 16) % 2 - (c // 16) % 2 - r // 64).astype(F32) * np.float32(0.25)
    turn = own_u * (c % 8 + 8 * (c // 64)).astype(F32) * inverse + quarter
    turn = turn - jnp.floor(turn + 0.5)
    same = (w_r == w_c) & ((r // 8) % 2 == (c // 8) % 2)
    tt[0:128, :], tt[128:256, :] = in_two(
        jnp.where(same, np.float32(1.0 / math.sqrt(nmx * 2 * cx)) * cos_turn(turn), zero)
    )

    width = 8 * nmx
    r = lax.broadcasted_iota(jnp.int32, (64, width), 0)
    c = lax.broadcasted_iota(jnp.int32, (64, width), 1)
    own_u = (r % 8).astype(F32) + (mxf * np.float32(8) - np.float32(U // 2))
    parts = U // (2 * cx)
    q = (5 + r // 32).astype(F32) + 2 * dzf
    inverse = jnp.where(
        r // 32 == 0,
        jnp.where(dz == 0, np.float32(1.0 / (parts * 5)), np.float32(1.0 / (parts * 7))),
        jnp.where(dz == 0, np.float32(1.0 / (parts * 6)), np.float32(1.0 / (parts * 8))),
    )
    turn = fold(own_u * ((c // 8).astype(F32) - np.float32(nmx // 2)), q * np.float32(parts), inverse)
    ff[0] = cos_turn(turn)
    ff[1] = -sin_turn(turn)

    for load in loads:
        load.wait()
    pl.semaphore_wait(barrier, len(peers))

    def remote(src, dst, send, recv, device):
        return pltpu.make_async_remote_copy(
            src_ref=src, dst_ref=dst, send_sem=send, recv_sem=recv, device_id=device, device_id_type=MESH
        )

    swaps = [
        remote(
            src.at[(*lead, slice(None), far_x)], dst.at[(*lead, own_z)], swap_send.at[i], swap_recv.at[i], partner
        )
        for i, (src, dst, lead) in enumerate(blocks_in)
    ]
    for swap in swaps:
        swap.start()

    def spread(i):
        for far in (1 << i, -(1 << i)):
            to_x, to_y = lax.rem(mx + far + 2 * nmx, nmx), lax.rem(my + far + 2 * nmy, nmy)
            pl.semaphore_signal(known.at[0, i], inc=1, device_id=(to_x, my, dz), device_id_type=MESH)
            pl.semaphore_signal(known.at[1, i], inc=1, device_id=(mx, to_y, dz), device_id_type=MESH)

    def heard(i):
        pl.semaphore_wait(known.at[0, i], 2)
        pl.semaphore_wait(known.at[1, i], 2)

    spread(0)
    swaps[0].wait()

    def constants(z, carry):
        kind = mat[z]
        for i in range(6):
            t = coef_table[i]
            coef[i, z] = jnp.where(kind < 2, jnp.where(kind == 0, t[0], t[1]), jnp.where(kind == 2, t[2], t[3]))
        return carry

    layers(constants, 0)
    for swap in swaps[1:]:
        swap.wait()

    def two_steps(r, carry):
        begin_round(r)
        sent = messages(r)
        for m in sent:
            m.start()
        for m in sent:
            m.wait()

        @pl.when(r == 0)
        def _():
            heard(0)
            spread(1)

        @pl.when(r == 1)
        def _():
            heard(1)
            spread(2)

        finish_round(r)
        return carry

    lax.fori_loop(0, STEPS // 2, two_steps, 0)

    blocks_out = (
        (e, e_out, (slice(None),)),
        (h, h_out, (slice(None),)),
        (pq, p_out, (slice(None), slice(None))),
    )
    stores = [
        pltpu.make_async_copy(src.at[(*lead, own_z)], dst.at[(*lead, slice(None), own_x)], out_sem.at[i])
        for i, (src, dst, lead) in enumerate(blocks_out)
    ]
    stores += [
        remote(
            src.at[(*lead, far_z)], dst.at[(*lead, slice(None), own_x)], back_send.at[i], back_recv.at[i], partner
        )
        for i, (src, dst, lead) in enumerate(blocks_out)
    ]

    def turned(w, what):
        found = []
        for n in range(1, STEPS + 1):
            found.append(np.float32(what(2 * math.pi * n / (8 + 2 * w))))
        return found

    def along_y(w, carry):
        cos_t, sin_t = turned(w, math.cos), turned(w, math.sin)
        re, im = [], []
        for p in range(2):
            re.append(sum(cos_t[n] * ps[n, p] for n in range(STEPS)))
            im.append(-sum(sin_t[n] * ps[n, p] for n in range(STEPS)))
        re, im = jnp.concatenate(re, 0), jnp.concatenate(im, 0)
        rows = jnp.concatenate([jnp.concatenate([re, -im], 1), jnp.concatenate([im, re], 1)], 0)
        high, low = in_two(rows)
        at = pl.ds(w * 4 * cx, 4 * cx)
        both = matmul(jnp.concatenate([high, low], 0), bw_high[w])
        ct[at, :] = both[0 : 4 * cx] + both[4 * cx : 8 * cx] + matmul(high, bw_low[w])
        return carry

    for w in range(W):
        along_y(w, 0)
    cbuf[...] = jnp.transpose(ct[...]).reshape(nmy, 8, 128)

    def place(j, n):
        return j + 1

    def share(j):
        k = place(j, nmy)
        to_y = lax.rem(my + k, nmy)
        return remote(cbuf.at[to_y], ra.at[k], a_send.at[k], a_recv.at[k], (mx, to_y, dz)), ra.at[k]

    def spread_out(j):
        k = place(j, nmx)
        return remote(gbuf, gall.at[mx], b_send.at[k], b_recv.at[k], (lax.rem(mx + k, nmx), my, dz))

    heard(2)

    for j in range(nmy - 1):
        share(j)[0].start()

    for store in stores:
        store.start()

    def arrived(j, total):
        copy, landed = share(j)
        copy.wait()
        return total + landed[...]

    total = cbuf[my]
    for j in range(nmy - 1):
        total = arrived(j, total)
    own[...] = total
    pair = remote(own, other, p_send.at[0], p_recv.at[0], partner)
    pair.start()
    pair.wait()
    mine = lax.broadcasted_iota(jnp.int32, (8, 128), 1) // 64 == dz
    total = jnp.where(mine, total, pltpu.roll(other[...], 64, axis=1))
    gbuf[...] = total
    gall[mx] = total

    for j in range(nmx - 1):
        spread_out(j).start()

    for j in range(nmx - 1):
        spread_out(j).wait()

    high, low = in_two(gall[...].reshape(width, 128))
    both = matmul(tt[...], high)
    both = both[0:128] + both[128:256] + matmul(tt[0:128, :], low)
    far = both[0:64] * ff[0] + both[64:128] * ff[1]
    shift = 8
    while shift < width:
        far = far + pltpu.roll(far, shift, axis=1)
        shift *= 2
    far = far.reshape(2, 2, 2, 8, width)
    fbuf[...] = far[..., 0:8]
    last = pltpu.make_async_copy(fbuf, f_out, out_sem.at[3])
    last.start()
    for store in stores:
        store.wait()
    last.wait()


def hand_over(*refs):
    copies = [pltpu.make_async_copy(a, b, refs[8].at[i]) for i, (a, b) in enumerate(zip(refs[:4], refs[4:8]))]
    for copy in copies:
        copy.start()
    for copy in copies:
        copy.wait()


def body(nmx, nmy, electric, magnetic, poles, material, exit_layer):
    near, cx, cy = material.shape
    depth, mine = 2 * near, cx // 2
    vm = lambda *shape: pltpu.VMEM(shape, F32)
    dma = lambda *shape: pltpu.SemaphoreType.DMA(shape)
    anywhere = pl.BlockSpec(memory_space=pl.ANY)
    field = (3, near, cx, cy)
    held = (3, depth, mine, cy)
    share = (2, 2, 2, U // nmx, V // nmy)
    electric, magnetic, poles, material = (
        pltpu.with_memory_space_constraint(x, pltpu.HBM) for x in (electric, magnetic, poles, material)
    )
    n = STEPS // 2
    outs = pl.pallas_call(
        functools.partial(kernel, nmx, nmy),
        out_shape=(
            jax.ShapeDtypeStruct(field, F32),
            jax.ShapeDtypeStruct(field, F32),
            jax.ShapeDtypeStruct((3, *field), F32),
            jax.ShapeDtypeStruct(share, F32),
        ),
        in_specs=[pl.BlockSpec(memory_space=pltpu.HBM)] * 4 + [pl.BlockSpec(memory_space=pltpu.SMEM)],
        out_specs=[anywhere] * 4,
        scratch_shapes=[
            vm(3, depth + 1, mine, cy), vm(*held), vm(*held), vm(*held), vm(3, *held),
            pltpu.VMEM((depth, mine, cy), jnp.int32), vm(6, depth, mine, cy),
            vm(n, 6, depth, cy), vm(n, 5, depth, cy), vm(n, mine, cy), vm(n, mine, cy),
            vm(n, 6, depth, cy), vm(n, 5, depth, cy), vm(n, 5, mine, cy), vm(n, 3, mine, cy),
            vm(2, depth, cy), vm(2, depth, cy), vm(2, depth, cy), vm(STEPS, 2, mine, cy),
            vm(128, V), *[pltpu.VMEM((W, V, 2 * cy), jnp.bfloat16)] * 2,
            pltpu.VMEM((256, 128), jnp.bfloat16), vm(2, 64, 8 * nmx),
            vm(nmy, 8, 128), vm(nmy, 8, 128), vm(8, 128), vm(8, 128), vm(8, 128), vm(nmx, 8, 128), vm(*share),
            dma(4), dma(4), dma(4), dma(4), dma(3), dma(3), pltpu.SemaphoreType.REGULAR((2, 3)),
            dma(n, 10), dma(n, 10), dma(1), dma(1), dma(nmy), dma(nmy), dma(nmx), dma(nmx),
        ],
        compiler_params=pltpu.CompilerParams(collective_id=0, has_side_effects=True, vmem_limit_bytes=24 * 2**20),
    )(electric, magnetic, poles, material, exit_layer)
    shapes = (field, field, (3, *field), share)
    return pl.pallas_call(
        hand_over,
        out_shape=tuple(jax.ShapeDtypeStruct(shape, F32) for shape in shapes),
        in_specs=[anywhere] * 4,
        out_specs=[pl.BlockSpec(memory_space=pltpu.HBM)] * 4,
        scratch_shapes=[dma(4)],
        compiler_params=pltpu.CompilerParams(vmem_limit_bytes=2**20),
    )(*outs)


def solution(mesh):
    nmx, nmy = mesh.shape["mx"], mesh.shape["my"]
    return jax.shard_map(
        functools.partial(body, nmx, nmy),
        mesh=mesh,
        in_specs=(
            P(None, "dz", "mx", "my"),
            P(None, "dz", "mx", "my"),
            P(None, None, "dz", "mx", "my"),
            P("dz", "mx", "my"),
            P(),
        ),
        out_specs=(
            P(None, "dz", "mx", "my"),
            P(None, "dz", "mx", "my"),
            P(None, None, "dz", "mx", "my"),
            P("dz", None, None, "mx", "my"),
        ),
        check_vma=False,
    )
```

```python
import functools
import math

import jax
import jax.numpy as jnp
import numpy as np
from jax import lax
from jax.experimental import pallas as pl
from jax.experimental.pallas import tpu as pltpu
from jax.sharding import PartitionSpec as P

STEPS = 4
W = 4
U = 128
V = 128
MESH = pl.DeviceIdType.MESH
F32 = jnp.float32

time_step = 0.5
eps_inf = np.array([1.0, 4.0, 2.1, 1.5])
drude_plasma = np.array([0.0, 0.0, 0.0, 2.0])
drude_damping = np.array([0.0, 0.0, 0.0, 0.1])
lorentz_square = np.array([0.3, 0.8, 1.0, 0.5])
lorentz_strength = np.array([0.0, 1.5, 0.1, 0.8])
lorentz_damping = np.array([0.0, 0.05, 0.02, 0.2])
drude_keep = (1.0 - drude_damping * time_step / 2) / (1.0 + drude_damping * time_step / 2)
drude_drive = drude_plasma * time_step / (1.0 + drude_damping * time_step / 2)
lorentz_keep = (1.0 - lorentz_damping * time_step / 2) / (1.0 + lorentz_damping * time_step / 2)
lorentz_push = time_step / (1.0 + lorentz_damping * time_step / 2)
coef_table = np.stack(
    [
        drude_keep,
        drude_drive,
        lorentz_keep,
        lorentz_push * lorentz_square * lorentz_strength,
        lorentz_push * lorentz_square,
        time_step / eps_inf,
    ]
).astype(np.float32)
DT = np.float32(time_step)

COS_TERMS = [np.float32((-1) ** k * (2 * math.pi) ** (2 * k) / math.factorial(2 * k)) for k in range(11)]
SIN_TERMS = [np.float32((-1) ** k * (2 * math.pi) ** (2 * k + 1) / math.factorial(2 * k + 1)) for k in range(11)]


GROUP = 8


def poly(terms, z):
    value = jnp.full_like(z, terms[-1])
    for term in terms[-2::-1]:
        value = value * z + term
    return value


def cos_turn(t):
    return poly(COS_TERMS, t * t)


def sin_turn(t):
    return t * poly(SIN_TERMS, t * t)


def in_two(x):
    high = x.astype(jnp.bfloat16)
    return high, (x - high.astype(F32)).astype(jnp.bfloat16)


def matmul(a, b):
    return lax.dot_general(a, b, (((1,), (1,)), ((), ())), preferred_element_type=F32)


def fold(product, period, inverse):
    left = product - jnp.floor(product * inverse + 0.5) * period
    return left * inverse


def kernel(
    nmx, nmy,
    e_in, h_in, p_in, m_in, exit_ref,
    e_out, h_out, p_out, f_out,
    e, h, hp, eb, pq, mat, coef,
    xu, xd, yd, yu, xu_in, xd_in, yd_in, yu_in, gx, hs, es, ps,
    ct, bw_high, bw_low, tt, ff, cbuf, cut, ra, gbuf, gall, fbuf,
    in_sem, out_sem, swap_send, swap_recv, back_send, back_recv, known, word,
    s_send, s_recv, a_send, a_recv, b_send, b_recv,
):
    depth, cx, cy = mat.shape
    half = depth // 2
    mx, my, dz = lax.axis_index("mx"), lax.axis_index("my"), lax.axis_index("dz")
    partner = (mx, my, 1 - dz)
    up_m, down_m = lax.rem(mx + 1, nmx), lax.rem(mx + nmx - 1, nmx)
    up_y, down_y = lax.rem(my + 1, nmy), lax.rem(my + nmy - 1, nmy)
    right, left = lax.rem(mx + dz, nmx), lax.rem(mx + dz + nmx - 1, nmx)

    own_z, own_x = pl.ds(pl.multiple_of(half * dz, half), half), pl.ds(pl.multiple_of(cx * dz, cx), cx)
    far_z, far_x = pl.ds(pl.multiple_of(half - half * dz, half), half), pl.ds(pl.multiple_of(cx - cx * dz, cx), cx)
    blocks_in = (
        (m_in, mat, ()),
        (e_in, e, (slice(None),)),
        (h_in, h, (slice(None),)),
        (p_in, pq, (slice(None), slice(None))),
    )
    loads = [
        pltpu.make_async_copy(src.at[(*lead, slice(None), own_x)], dst.at[(*lead, own_z)], in_sem.at[i])
        for i, (src, dst, lead) in enumerate(blocks_in)
    ]
    for load in loads:
        load.start()

    barrier = pltpu.get_barrier_semaphore()
    peers = [(up_m, my, dz), (down_m, my, dz), (mx, up_y, dz), (mx, down_y, dz)]
    peers += [(right, my, 1 - dz), (left, my, 1 - dz)]
    for peer in peers:
        pl.semaphore_signal(barrier, inc=1, device_id=peer, device_id_type=MESH)

    one, zero = np.float32(1.0), np.float32(0.0)
    place_x = 2 * mx + dz
    xp, xm = jnp.where(place_x < 2 * nmx - 1, one, zero), jnp.where(place_x > 0, one, zero)
    yp, ym = jnp.where(my < nmy - 1, one, zero), jnp.where(my > 0, one, zero)

    lane = lax.broadcasted_iota(jnp.int32, (cx, cy), 1)
    row = lax.broadcasted_iota(jnp.int32, (cx, cy), 0)
    at_lane0, at_lane_end = lane == 0, lane == cy - 1
    at_row0, at_row_end = row == 0, row == cx - 1
    slab_lane = lax.broadcasted_iota(jnp.int32, (depth, cy), 1)
    slab_row = lax.broadcasted_iota(jnp.int32, (depth, cy), 0)
    slab_lane0, slab_lane_end = slab_lane == 0, slab_lane == cy - 1
    nothing = jnp.zeros((cx, cy), F32)
    slab_nothing = jnp.zeros((depth, cy), F32)

    def to(x, src, dst):
        shift = (dst - src + cy) % cy
        return pltpu.roll(x, shift, axis=1) if not isinstance(shift, int) or shift else x

    def layers(body, carry):
        def some(g, carry):
            for j in range(GROUP):
                carry = body(GROUP * g + j, carry)
            return carry

        return lax.fori_loop(0, depth // GROUP, some, carry)

    def y_next(x):
        return pltpu.roll(x, cy - 1, axis=1)

    def y_last(x):
        return pltpu.roll(x, 1, axis=1)

    def x_next(x):
        return pltpu.roll(x, cx - 1, axis=0)

    def x_last(x):
        return pltpu.roll(x, 1, axis=0)

    def wide(x):
        return jnp.broadcast_to(x, (cx, cy))

    def slot(tile, which):
        return to(tile, which * depth, 0)

    def tile_up(x):
        lanes = lax.broadcasted_iota(jnp.int32, x.shape, 1)
        return jnp.where(lanes == depth - 1, zero, y_next(x)) - x

    def tile_down(x):
        lanes = lax.broadcasted_iota(jnp.int32, x.shape, 1)
        return x - jnp.where(lanes == 0, zero, y_last(x))

    def slab_up(x):
        return jnp.where(slab_row == depth - 1, zero, pltpu.roll(x, depth - 1, axis=0)) - x

    def slab_down(x):
        return x - jnp.where(slab_row == 0, zero, pltpu.roll(x, 1, axis=0))

    def column(x):
        picked = jnp.where(slab_lane == slab_row, jnp.broadcast_to(x, (depth, cy)), slab_nothing)
        return jnp.sum(picked, axis=1, keepdims=True)

    def at_end(x):
        return jnp.where(slab_lane_end, column(x), slab_nothing)

    def at_start(x):
        return jnp.where(slab_lane0, column(x), slab_nothing)

    def poles_of(z, fields):
        keep_d, drive_d, keep_l, drive_l, restore_l, scale = [coef[i, z] for i in range(6)]
        rest = []
        for c, field in enumerate(fields):
            polar, current, drude = pq[0, c, z], pq[1, c, z], pq[2, c, z]
            current_new = keep_l * current + drive_l * field - restore_l * polar
            drude_new = keep_d * drude + drive_d * field
            pq[0, c, z] = polar + DT * current_new
            pq[1, c, z] = current_new
            pq[2, c, z] = drude_new
            rest.append(field - scale * (0.5 * (drude + drude_new) + current_new))
        return rest, scale

    def begin_round(r):
        def layer(z, carry):
            low_tile, high_tile, hx_below, hy_below = carry
            ex, ey, ez = e[0, z], e[1, z], e[2, z]
            exn, eyn = e[0, z + 1], e[1, z + 1]
            dy_ez = jnp.where(at_lane_end, nothing, y_next(ez)) - ez
            dy_ex = jnp.where(at_lane_end, nothing, y_next(ex)) - ex
            dx_ez = jnp.where(at_row_end, nothing, x_next(ez)) - ez
            dx_ey = jnp.where(at_row_end, nothing, x_next(ey)) - ey
            hx = h[0, z] - DT * (dy_ez - (eyn - ey))
            hy = h[1, z] - DT * ((exn - ex) - dx_ez)
            hz = h[2, z] - DT * (dx_ey - dy_ex)
            hp[0, z], hp[1, z], hp[2, z] = hx, hy, hz
            rest, scale = poles_of(z, (ex, ey, ez))
            eb[0, z], eb[1, z], eb[2, z] = rest
            dx_hy = hy - jnp.where(at_row0, nothing, x_last(hy))
            dx_hz = hz - jnp.where(at_row0, nothing, x_last(hz))
            dy_hx = hx - jnp.where(at_lane0, nothing, y_last(hx))
            dy_hz = hz - jnp.where(at_lane0, nothing, y_last(hz))
            px = rest[0] + scale * (dy_hz - (hy - hy_below))
            py = rest[1] + scale * ((hx - hx_below) - dx_hz)
            pz = rest[2] + scale * (dx_hy - dy_hx)
            for i, x in enumerate((hy, hz, px, py, pz, scale)):
                xu[r, i, pl.ds(z, 1), :] = x[cx - 1 : cx]
            for i, x in enumerate((ey, ez, py, pz, scale)):
                xd[r, i, pl.ds(z, 1), :] = x[0:1]
            for i, x in enumerate((ex, ez, px, pz, scale, ey, hy)):
                low_tile = jnp.where(lane == i * depth + z, to(x, 0, i * depth + z), low_tile)
            mixed = jnp.where(at_row0, ez, jnp.where(row == 1, x_last(y_last(ey)), hy))
            for i, x in enumerate((hx, hz, px, py, pz, scale, ey, mixed)):
                high_tile = jnp.where(lane == i * depth + z, to(x, cy - 1, i * depth + z), high_tile)
            return low_tile, high_tile, hx, hy

        low_tile, high_tile, _, _ = layers(layer, (nothing,) * 4)
        yd[r] = low_tile
        yu[r] = high_tile

    def messages(r):
        there = 1 - dz
        table = (
            (yd.at[r], yd_in.at[r, 1], (right, down_y, there)),
            (yu.at[r], yu_in.at[r, 1], (left, up_y, there)),
            (yd.at[r], yd_in.at[r, 2], (left, down_y, there)),
            (yu.at[r], yu_in.at[r, 2], (right, up_y, there)),
            (xu.at[r, pl.ds(0, 6 - r)], xu_in.at[r, pl.ds(0, 6 - r)], (right, my, there)),
            (xd.at[r, pl.ds(0, 5 - r)], xd_in.at[r, pl.ds(0, 5 - r)], (left, my, there)),
            (yd.at[r], yd_in.at[r, 3], (right, my, there)),
            (yd.at[r], yd_in.at[r, 4], (left, my, there)),
            (yd.at[r], yd_in.at[r, 0], (mx, down_y, dz)),
            (yu.at[r], yu_in.at[r, 0], (mx, up_y, dz)),
        )
        copies = [
            pltpu.make_async_remote_copy(
                src_ref=src, dst_ref=dst, send_sem=s_send.at[r, k], recv_sem=s_recv.at[r, k],
                device_id=device, device_id_type=MESH,
            )
            for k, (src, dst, device) in enumerate(table)
        ]
        return copies[:4], copies[4:]

    def electric_at(z, fields, below, hx_ym, hz_ym, rest, scale):
        hx, hy, hz = fields
        dx_hy = hy - jnp.where(at_row0, wide(gx[0, pl.ds(z, 1), :]), x_last(hy))
        dx_hz = hz - jnp.where(at_row0, wide(gx[1, pl.ds(z, 1), :]), x_last(hz))
        dy_hx = hx - jnp.where(at_lane0, to(hx_ym, z, 0), y_last(hx))
        dy_hz = hz - jnp.where(at_lane0, to(hz_ym, z, 0), y_last(hz))
        ex = rest[0] + scale * (dy_hz - (hy - below[1]))
        ey = rest[1] + scale * ((hx - below[0]) - dx_hz)
        ez = rest[2] + scale * (dx_hy - dy_hx)
        return ex, ey, ez

    def here_of(z):
        return jnp.where(exit_ref[0] == z, one, zero)

    def finish_round(r):
        own_low = yd[r]
        top = yd_in[r, 0] * yp
        left_top, right_top = yd_in[r, 1] * (xm * yp), yd_in[r, 2] * (xp * yp)
        left_low, right_low = yd_in[r, 3] * xm, yd_in[r, 4] * xp
        bottom = yu_in[r, 0] * ym
        right_bottom, left_bottom = yu_in[r, 1] * (xp * ym), yu_in[r, 2] * (xm * ym)
        end = cx - 1
        lt = left_top[end : end + 1]
        lt_ex, lt_ez, lt_px, lt_scale, lt_hy = [slot(lt, i) for i in (0, 1, 2, 4, 6)]
        lt_ex2 = left_top[end - 1 : end]
        rb = right_bottom[0:1]
        rb_hx, rb_py, rb_scale, rb_ey, rb_ez = [slot(rb, i) for i in (0, 3, 5, 6, 7)]
        rb_ey2 = slot(right_bottom[1:2], 7)
        lb = left_bottom[end : end + 1]
        lb_hx, lb_hz, lb_hy = [slot(lb, i) for i in (0, 1, 7)]
        rt = right_top[0:1]
        rt_ex, rt_ez, rt_ey = [slot(rt, i) for i in (0, 1, 5)]
        l_ex, l_ez = [slot(left_low[end : end + 1], i) for i in (0, 1)]
        r_ex, r_ez = [slot(right_low[0:1], i) for i in (0, 1)]
        t_ez, t_ey = [slot(top[0:1], i) for i in (1, 5)]
        b_ey, b_ez = slot(bottom[0:1], 6), slot(bottom[0:1], 7)

        corner_hx = (lb_hx - DT * l_ez) * (xm * ym)
        corner_hy = (lb_hy + DT * b_ez) * (xm * ym)
        corner_hz = (lb_hz - DT * b_ey + DT * l_ex) * (xm * ym)
        rb_hx = (rb_hx - DT * r_ez) * (xp * ym)
        lt_hy = (lt_hy + DT * t_ez) * (xm * yp)
        lt_ex_end = at_end(DT * lt_ex)
        more_hy_x = DT * xd[r, 1]
        more_hz_x = lt_ex_end - DT * xd[r, 0]
        hy_x = (xu_in[r, 0] + more_hy_x) * xm
        hz_x = (xu_in[r, 1] + more_hz_x) * xm
        more_hx_y = -DT * slot(own_low, 1)
        more_hz_y = DT * slot(own_low, 0) - jnp.where(at_row_end, DT * rb_ey, nothing)
        hx_y = (bottom + more_hx_y) * ym
        hz_y = (slot(bottom, 1) + more_hz_y) * ym
        gx[0], gx[1] = hy_x, hz_x

        def first(z, carry):
            below, plane, ex_low, ez_low, hx_high, hz_high = carry
            hx, hy, hz = hp[0, z], hp[1, z], hp[2, z]
            hy = hy + jnp.where(at_row_end, wide(xd_in[r, 1, pl.ds(z, 1), :] * (DT * xp)), nothing)
            hz = hz - jnp.where(at_row_end, wide(xd_in[r, 0, pl.ds(z, 1), :] * (DT * xp)), nothing)
            hx = hx - jnp.where(at_lane_end, DT * to(top, depth + z, cy - 1), nothing)
            hz = hz + jnp.where(at_lane_end, DT * to(top, z, cy - 1), nothing)
            h[0, z], h[1, z], h[2, z] = hx, hy, hz
            fields = electric_at(z, (hx, hy, hz), below, hx_y, hz_y, (eb[0, z], eb[1, z], eb[2, z]), coef[5, z])
            ex, ey, ez = fields
            e[0, z], e[1, z], e[2, z] = fields
            rest, _ = poles_of(z, fields)
            eb[0, z], eb[1, z], eb[2, z] = rest
            here = here_of(z)
            plane = (plane[0] + here * ex, plane[1] + here * ey)
            hs[0, pl.ds(z, 1), :] = hy[cx - 1 : cx]
            hs[1, pl.ds(z, 1), :] = hz[cx - 1 : cx]
            es[0, pl.ds(z, 1), :] = ey[0:1]
            es[1, pl.ds(z, 1), :] = ez[0:1]
            ex_low = jnp.where(lane == z, to(ex, 0, z), ex_low)
            ez_low = jnp.where(lane == z, to(ez, 0, z), ez_low)
            hx_high = jnp.where(lane == z, to(hx, cy - 1, z), hx_high)
            hz_high = jnp.where(lane == z, to(hz, cy - 1, z), hz_high)
            return (hx, hy), plane, ex_low, ez_low, hx_high, hz_high

        pair = (nothing, nothing)
        _, plane, ex_low, ez_low, hx_high, hz_high = layers(first, (pair, pair, *pair, *pair))
        ps[2 * r, 0], ps[2 * r, 1] = plane

        more_hx = at_end(-DT * rt_ez)
        more_hz = at_end(DT * rt_ex)
        scale = xd_in[0, 4] * xp
        ey_right = xd_in[r, 2] * xp + scale * (slab_down(more_hx) - more_hz + hs[1])
        ez_right = xd_in[r, 3] * xp + scale * (at_start(rb_hx) - hs[0] - more_hx)
        gx_e = (ey_right, ez_right)

        more_hx = at_end(-DT * lt_ez)
        scale = xu_in[0, 5]
        hz_shift = jnp.where(slab_lane0, column(corner_hz), pltpu.roll(more_hz_x, 1, axis=1))
        ex_left = xu_in[r, 2] + scale * (more_hz_x - hz_shift - slab_down(more_hy_x))
        ey_left = xu_in[r, 3] + scale * (slab_down(more_hx) - (more_hz_x - at_end(DT * lt_ex2)))
        ez_left = xu_in[r, 4] + scale * (more_hy_x - more_hx + at_start(corner_hx))
        lt_more = column(-DT * t_ey - tile_down(DT * t_ez))
        ex_lt = column(lt_px) + column(lt_scale) * (lt_more - hz_x)

        more_hy = jnp.where(at_row_end, DT * rt_ez, nothing)
        more_hz = jnp.where(at_row_end, -DT * rt_ey, nothing)
        scale = slot(top, 4)
        ex_top = slot(top, 2) + scale * (more_hz - hz_high - tile_down(more_hy))
        ez_top = slot(top, 3) + scale * (more_hy - jnp.where(at_row0, lt_hy, nothing) + hx_high)

        more_hy = jnp.where(at_row_end, DT * rb_ez, nothing)
        scale = slot(bottom, 5)
        hz_two = jnp.where(at_row_end, -DT * rb_ey2, nothing)
        ex_bottom = slot(bottom, 2) + scale * (more_hz_y - hz_two - tile_down(more_hy))
        hz_shift = jnp.where(at_row0, wide(corner_hz), x_last(more_hz_y))
        ey_bottom = slot(bottom, 3) + scale * (tile_down(more_hx_y) - (more_hz_y - hz_shift))
        ez_bottom = slot(bottom, 4) + scale * (more_hy - jnp.where(at_row0, corner_hy, nothing) - more_hx_y)
        ey_rb = rb_py + rb_scale * (hz_y[end : end + 1] - DT * r_ex - tile_down(DT * r_ez))

        gx[0] = (hy_x - DT * (slab_up(ex_left) - (es[1] - ez_left))) * xm
        ex_next = jnp.where(slab_lane_end, ex_lt, pltpu.roll(ex_left, cy - 1, axis=1))
        gx[1] = (hz_x - DT * ((es[0] - ey_left) - (ex_next - ex_left))) * xm
        hx_y = (hx_y - DT * ((ez_low - ez_bottom) - tile_up(ey_bottom))) * ym
        ey_next = jnp.where(at_row_end, wide(ey_rb), x_next(ey_bottom))
        hz_y = (hz_y - DT * ((ey_next - ey_bottom) - (ex_low - ex_bottom))) * ym
        hs[0], hs[1] = gx_e

        def second(z, carry):
            below, plane = carry
            ex, ey, ez = e[0, z], e[1, z], e[2, z]
            exn, eyn = e[0, z + 1], e[1, z + 1]
            dy_ez = jnp.where(at_lane_end, to(ez_top, z, cy - 1), y_next(ez)) - ez
            dy_ex = jnp.where(at_lane_end, to(ex_top, z, cy - 1), y_next(ex)) - ex
            dx_ez = jnp.where(at_row_end, wide(hs[1, pl.ds(z, 1), :]), x_next(ez)) - ez
            dx_ey = jnp.where(at_row_end, wide(hs[0, pl.ds(z, 1), :]), x_next(ey)) - ey
            hx = h[0, z] - DT * (dy_ez - (eyn - ey))
            hy = h[1, z] - DT * ((exn - ex) - dx_ez)
            hz = h[2, z] - DT * (dx_ey - dy_ex)
            h[0, z], h[1, z], h[2, z] = hx, hy, hz
            fields = electric_at(z, (hx, hy, hz), below, hx_y, hz_y, (eb[0, z], eb[1, z], eb[2, z]), coef[5, z])
            e[0, z], e[1, z], e[2, z] = fields
            here = here_of(z)
            return (hx, hy), (plane[0] + here * fields[0], plane[1] + here * fields[1])

        _, plane = layers(second, (pair, pair))
        ps[2 * r + 1, 0], ps[2 * r + 1, 1] = plane

    for i in range(3):
        e[i, depth] = nothing

    dzf, mxf, myf = dz.astype(F32), mx.astype(F32), my.astype(F32)
    vrow = lax.broadcasted_iota(jnp.int32, (V, cy), 0).astype(F32) - np.float32(V // 2)
    ypos = lax.broadcasted_iota(jnp.int32, (V, cy), 1).astype(F32) + (myf - np.float32(nmy // 2)) * np.float32(cy)
    size = np.float32(1.0 / math.sqrt(nmy * cy))
    for w in range(W):
        turn = fold(vrow * ypos, np.float32(V * (5 + w)), np.float32(1.0 / (V * (5 + w))))
        bw_high[w, :, 0:cy], bw_low[w, :, 0:cy] = in_two(size * cos_turn(turn))
        bw_high[w, :, cy : 2 * cy], bw_low[w, :, cy : 2 * cy] = in_two(-size * sin_turn(turn))

    r = lax.broadcasted_iota(jnp.int32, (128, 128), 0)
    c = lax.broadcasted_iota(jnp.int32, (128, 128), 1)
    w_r, w_c = (r // 32) % 2, (c // 32) % 2
    own_u = (r % 8).astype(F32) + (mxf * np.float32(8) - np.float32(U // 2))
    inverse = jnp.where(
        w_r == 0,
        jnp.where(dz == 0, np.float32(1.0 / (U * 5)), np.float32(1.0 / (U * 7))),
        jnp.where(dz == 0, np.float32(1.0 / (U * 6)), np.float32(1.0 / (U * 8))),
    )
    quarter = ((r // 16) % 2 - (c // 16) % 2 - r // 64).astype(F32) * np.float32(0.25)
    turn = own_u * (c % 8 + 8 * (c // 64)).astype(F32) * inverse + quarter
    turn = turn - jnp.floor(turn + 0.5)
    same = (w_r == w_c) & ((r // 8) % 2 == (c // 8) % 2)
    tt[0:128, :], tt[128:256, :] = in_two(
        jnp.where(same, np.float32(1.0 / math.sqrt(nmx * 2 * cx)) * cos_turn(turn), zero)
    )

    width = 8 * nmx
    r = lax.broadcasted_iota(jnp.int32, (64, width), 0)
    c = lax.broadcasted_iota(jnp.int32, (64, width), 1)
    own_u = (r % 8).astype(F32) + (mxf * np.float32(8) - np.float32(U // 2))
    parts = U // (2 * cx)
    q = (5 + r // 32).astype(F32) + 2 * dzf
    inverse = jnp.where(
        r // 32 == 0,
        jnp.where(dz == 0, np.float32(1.0 / (parts * 5)), np.float32(1.0 / (parts * 7))),
        jnp.where(dz == 0, np.float32(1.0 / (parts * 6)), np.float32(1.0 / (parts * 8))),
    )
    turn = fold(own_u * ((c // 8).astype(F32) - np.float32(nmx // 2)), q * np.float32(parts), inverse)
    ff[0] = cos_turn(turn)
    ff[1] = -sin_turn(turn)

    for load in loads:
        load.wait()
    pl.semaphore_wait(barrier, len(peers))

    def remote(src, dst, send, recv, device):
        return pltpu.make_async_remote_copy(
            src_ref=src, dst_ref=dst, send_sem=send, recv_sem=recv, device_id=device, device_id_type=MESH
        )

    swaps = [
        remote(
            src.at[(*lead, slice(None), far_x)], dst.at[(*lead, own_z)], swap_send.at[i], swap_recv.at[i], partner
        )
        for i, (src, dst, lead) in enumerate(blocks_in)
    ]
    for swap in swaps:
        swap.start()

    def spread(i):
        for far in (1 << i, -(1 << i)):
            to_x, to_y = lax.rem(mx + far + 2 * nmx, nmx), lax.rem(my + far + 2 * nmy, nmy)
            pl.semaphore_signal(known.at[0, i], inc=1, device_id=(to_x, my, dz), device_id_type=MESH)
            pl.semaphore_signal(known.at[1, i], inc=1, device_id=(mx, to_y, dz), device_id_type=MESH)

    def heard(i):
        pl.semaphore_wait(known.at[0, i], 2)
        pl.semaphore_wait(known.at[1, i], 2)

    spread(0)
    swaps[0].wait()

    def constants(z, carry):
        kind = mat[z]
        for i in range(6):
            t = coef_table[i]
            coef[i, z] = jnp.where(kind < 2, jnp.where(kind == 0, t[0], t[1]), jnp.where(kind == 2, t[2], t[3]))
        return carry

    layers(constants, 0)
    for swap in swaps[1:]:
        swap.wait()

    def two_steps(r, carry):
        begin_round(r)

        @pl.when(r == 0)
        def _():
            diagonal, straight = messages(0)
            for m in straight:
                m.start()
            pl.semaphore_wait(known.at[1, 0], 2)
            for m in diagonal:
                m.start()
            pl.semaphore_wait(known.at[0, 0], 2)
            spread(1)
            for m in straight + diagonal:
                m.wait()

        @pl.when(r == 1)
        def _():
            diagonal, straight = messages(1)
            for m in diagonal + straight:
                m.start()
            heard(1)
            spread(2)
            for m in straight + diagonal:
                m.wait()

        finish_round(r)
        return carry

    lax.fori_loop(0, STEPS // 2, two_steps, 0)

    blocks_out = (
        (e, e_out, (slice(None),)),
        (h, h_out, (slice(None),)),
        (pq, p_out, (slice(None), slice(None))),
    )
    stores = [
        pltpu.make_async_copy(src.at[(*lead, own_z)], dst.at[(*lead, slice(None), own_x)], out_sem.at[i])
        for i, (src, dst, lead) in enumerate(blocks_out)
    ]
    stores += [
        remote(
            src.at[(*lead, far_z)], dst.at[(*lead, slice(None), own_x)], back_send.at[i], back_recv.at[i], partner
        )
        for i, (src, dst, lead) in enumerate(blocks_out)
    ]

    def turned(w, what):
        found = []
        for n in range(1, STEPS + 1):
            found.append(np.float32(what(2 * math.pi * n / (8 + 2 * w))))
        return found

    def along_y(w, carry):
        cos_t, sin_t = turned(w, math.cos), turned(w, math.sin)
        re, im = [], []
        for p in range(2):
            re.append(sum(cos_t[n] * ps[n, p] for n in range(STEPS)))
            im.append(-sum(sin_t[n] * ps[n, p] for n in range(STEPS)))
        re, im = jnp.concatenate(re, 0), jnp.concatenate(im, 0)
        rows = jnp.concatenate([jnp.concatenate([re, -im], 1), jnp.concatenate([im, re], 1)], 0)
        high, low = in_two(rows)
        at = pl.ds(w * 4 * cx, 4 * cx)
        both = matmul(jnp.concatenate([high, low], 0), bw_high[w])
        ct[at, :] = both[0 : 4 * cx] + both[4 * cx : 8 * cx] + matmul(high, bw_low[w])
        return carry

    for w in range(W):
        along_y(w, 0)
    cbuf[...] = jnp.transpose(ct[...]).reshape(nmy, 8, 128)

    def place(j, n):
        return j + 1

    left_half = lax.broadcasted_iota(jnp.int32, (8, 128), 1) < 64
    for m in range(nmy):
        tile = cbuf[m]
        turned_tile = pltpu.roll(tile, 64, axis=1)
        cut[0, m] = jnp.where(left_half, tile, pltpu.roll(turned_tile, 4, axis=0))[0:4]
        cut[1, m] = jnp.where(left_half, turned_tile, pltpu.roll(tile, 4, axis=0))[0:4]

    def share(j, core):
        k = place(j, nmy)
        to_y = lax.rem(my + k, nmy)
        at = remote(
            cut.at[core, to_y], ra.at[dz, k], a_send.at[core, k], a_recv.at[dz, k], (mx, to_y, core)
        )
        return at

    def landing(j, core):
        k = place(j, nmy)
        return remote(cut.at[core, my], ra.at[core, k], a_send.at[core, k], a_recv.at[core, k], (mx, up_y, core))

    def spread_out(j):
        k = place(j, nmx)
        return remote(gbuf, gall.at[mx], b_send.at[k], b_recv.at[k], (lax.rem(mx + k, nmx), my, dz))

    pl.semaphore_wait(known.at[1, 2], 2)

    pair = remote(cut.at[1 - dz, my], ra.at[dz, 0], a_send.at[1 - dz, 0], a_recv.at[dz, 0], partner)
    pair_in = remote(cut.at[1 - dz, my], ra.at[1 - dz, 0], a_send.at[1 - dz, 0], a_recv.at[1 - dz, 0], partner)
    pl.semaphore_signal(word, inc=1, device_id=partner, device_id_type=MESH)
    for j in range(nmy - 1):
        share(j, dz).start()
        if j + 1 != nmy // 2:
            share(j, 1 - dz).start()
    pair.start()
    pl.semaphore_wait(word, 1)
    share(nmy // 2 - 1, 1 - dz).start()
    for store in stores:
        store.start()
    ra[dz, 0] = cut[dz, my]
    for core in range(2):
        for j in range(nmy - 1):
            landing(j, core).wait_recv()
    pair_in.wait_recv()
    sums = []
    for core in range(2):
        total = ra[core, 0]
        for k in range(1, nmy):
            total = total + ra[core, k]
        sums.append(total)
    half_row = left_half[0:4]
    top = jnp.where(half_row, sums[0], pltpu.roll(sums[1], 64, axis=1))
    low_rows = jnp.where(half_row, pltpu.roll(sums[0], 64, axis=1), sums[1])
    total = jnp.concatenate([top, low_rows], 0)
    gbuf[...] = total
    gall[mx] = total

    pl.semaphore_wait(known.at[0, 2], 2)
    for j in range(nmx - 1):
        spread_out(j).start()

    for j in range(nmx - 1):
        spread_out(j).wait()

    high, low = in_two(gall[...].reshape(width, 128))
    both = matmul(tt[...], high)
    both = both[0:128] + both[128:256] + matmul(tt[0:128, :], low)
    far = both[0:64] * ff[0] + both[64:128] * ff[1]
    shift = 8
    while shift < width:
        far = far + pltpu.roll(far, shift, axis=1)
        shift *= 2
    far = far.reshape(2, 2, 2, 8, width)
    fbuf[...] = far[..., 0:8]
    last = pltpu.make_async_copy(fbuf, f_out, out_sem.at[3])
    last.start()
    for j in range(nmy - 1):
        for core in range(2):
            share(j, core).wait_send()
    pair.wait_send()
    for store in stores:
        store.wait()
    last.wait()


def hand_over(*refs):
    copies = [pltpu.make_async_copy(a, b, refs[8].at[i]) for i, (a, b) in enumerate(zip(refs[:4], refs[4:8]))]
    for copy in copies:
        copy.start()
    for copy in copies:
        copy.wait()


def body(nmx, nmy, electric, magnetic, poles, material, exit_layer):
    near, cx, cy = material.shape
    depth, mine = 2 * near, cx // 2
    vm = lambda *shape: pltpu.VMEM(shape, F32)
    dma = lambda *shape: pltpu.SemaphoreType.DMA(shape)
    anywhere = pl.BlockSpec(memory_space=pl.ANY)
    field = (3, near, cx, cy)
    held = (3, depth, mine, cy)
    share = (2, 2, 2, U // nmx, V // nmy)
    electric, magnetic, poles, material = (
        pltpu.with_memory_space_constraint(x, pltpu.HBM) for x in (electric, magnetic, poles, material)
    )
    n = STEPS // 2
    outs = pl.pallas_call(
        functools.partial(kernel, nmx, nmy),
        out_shape=(
            jax.ShapeDtypeStruct(field, F32),
            jax.ShapeDtypeStruct(field, F32),
            jax.ShapeDtypeStruct((3, *field), F32),
            jax.ShapeDtypeStruct(share, F32),
        ),
        in_specs=[pl.BlockSpec(memory_space=pltpu.HBM)] * 4 + [pl.BlockSpec(memory_space=pltpu.SMEM)],
        out_specs=[anywhere] * 4,
        scratch_shapes=[
            vm(3, depth + 1, mine, cy), vm(*held), vm(*held), vm(*held), vm(3, *held),
            pltpu.VMEM((depth, mine, cy), jnp.int32), vm(6, depth, mine, cy),
            vm(n, 6, depth, cy), vm(n, 5, depth, cy), vm(n, mine, cy), vm(n, mine, cy),
            vm(n, 6, depth, cy), vm(n, 5, depth, cy), vm(n, 5, mine, cy), vm(n, 3, mine, cy),
            vm(2, depth, cy), vm(2, depth, cy), vm(2, depth, cy), vm(STEPS, 2, mine, cy),
            vm(128, V), *[pltpu.VMEM((W, V, 2 * cy), jnp.bfloat16)] * 2,
            pltpu.VMEM((256, 128), jnp.bfloat16), vm(2, 64, 8 * nmx),
            vm(nmy, 8, 128), vm(2, nmy, 4, 128), vm(2, nmy, 4, 128), vm(8, 128), vm(nmx, 8, 128), vm(*share),
            dma(4), dma(4), dma(4), dma(4), dma(3), dma(3), pltpu.SemaphoreType.REGULAR((2, 3)), pltpu.SemaphoreType.REGULAR,
            dma(n, 10), dma(n, 10), dma(2, nmy), dma(2, nmy), dma(nmx), dma(nmx),
        ],
        compiler_params=pltpu.CompilerParams(collective_id=0, has_side_effects=True, vmem_limit_bytes=24 * 2**20),
    )(electric, magnetic, poles, material, exit_layer)
    shapes = (field, field, (3, *field), share)
    return pl.pallas_call(
        hand_over,
        out_shape=tuple(jax.ShapeDtypeStruct(shape, F32) for shape in shapes),
        in_specs=[anywhere] * 4,
        out_specs=[pl.BlockSpec(memory_space=pltpu.HBM)] * 4,
        scratch_shapes=[dma(4)],
        compiler_params=pltpu.CompilerParams(vmem_limit_bytes=2**20),
    )(*outs)


def solution(mesh):
    nmx, nmy = mesh.shape["mx"], mesh.shape["my"]
    return jax.shard_map(
        functools.partial(body, nmx, nmy),
        mesh=mesh,
        in_specs=(
            P(None, "dz", "mx", "my"),
            P(None, "dz", "mx", "my"),
            P(None, None, "dz", "mx", "my"),
            P("dz", "mx", "my"),
            P(),
        ),
        out_specs=(
            P(None, "dz", "mx", "my"),
            P(None, "dz", "mx", "my"),
            P(None, None, "dz", "mx", "my"),
            P("dz", None, None, "mx", "my"),
        ),
        check_vma=False,
    )
```

```python
import functools
import math

import jax
import jax.numpy as jnp
import numpy as np
from jax import lax
from jax.experimental import pallas as pl
from jax.experimental.pallas import tpu as pltpu
from jax.sharding import PartitionSpec as P

STEPS = 4
W = 4
U = 128
V = 128
MESH = pl.DeviceIdType.MESH
F32 = jnp.float32

time_step = 0.5
eps_inf = np.array([1.0, 4.0, 2.1, 1.5])
drude_plasma = np.array([0.0, 0.0, 0.0, 2.0])
drude_damping = np.array([0.0, 0.0, 0.0, 0.1])
lorentz_square = np.array([0.3, 0.8, 1.0, 0.5])
lorentz_strength = np.array([0.0, 1.5, 0.1, 0.8])
lorentz_damping = np.array([0.0, 0.05, 0.02, 0.2])
drude_keep = (1.0 - drude_damping * time_step / 2) / (1.0 + drude_damping * time_step / 2)
drude_drive = drude_plasma * time_step / (1.0 + drude_damping * time_step / 2)
lorentz_keep = (1.0 - lorentz_damping * time_step / 2) / (1.0 + lorentz_damping * time_step / 2)
lorentz_push = time_step / (1.0 + lorentz_damping * time_step / 2)
coef_table = np.stack(
    [
        drude_keep,
        drude_drive,
        lorentz_keep,
        lorentz_push * lorentz_square * lorentz_strength,
        lorentz_push * lorentz_square,
        time_step / eps_inf,
    ]
).astype(np.float32)
DT = np.float32(time_step)

COS_TERMS = [np.float32((-1) ** k * (2 * math.pi) ** (2 * k) / math.factorial(2 * k)) for k in range(11)]
SIN_TERMS = [np.float32((-1) ** k * (2 * math.pi) ** (2 * k + 1) / math.factorial(2 * k + 1)) for k in range(11)]


GROUP = 8


def poly(terms, z):
    value = jnp.full_like(z, terms[-1])
    for term in terms[-2::-1]:
        value = value * z + term
    return value


def cos_turn(t):
    return poly(COS_TERMS, t * t)


def sin_turn(t):
    return t * poly(SIN_TERMS, t * t)


def in_two(x):
    high = x.astype(jnp.bfloat16)
    return high, (x - high.astype(F32)).astype(jnp.bfloat16)


def matmul(a, b):
    return lax.dot_general(a, b, (((1,), (1,)), ((), ())), preferred_element_type=F32)


def fold(product, period, inverse):
    left = product - jnp.floor(product * inverse + 0.5) * period
    return left * inverse


def kernel(
    nmx, nmy,
    e_in, h_in, p_in, m_in, exit_ref,
    e_out, h_out, p_out, f_out,
    e, h, hp, eb, pq, mat, coef,
    xu, xd, yd, yu, xu_in, xd_in, yd_in, yu_in, gx, hs, es, ps,
    ct, bw_high, bw_low, tt, ff, cbuf, cut, ra, gbuf, gall, fbuf,
    in_sem, out_sem, swap_send, swap_recv, back_send, back_recv, known, word,
    s_send, s_recv, a_send, a_recv, b_send, b_recv,
):
    depth, cx, cy = mat.shape
    half = depth // 2
    mx, my, dz = lax.axis_index("mx"), lax.axis_index("my"), lax.axis_index("dz")
    partner = (mx, my, 1 - dz)
    up_m, down_m = lax.rem(mx + 1, nmx), lax.rem(mx + nmx - 1, nmx)
    up_y, down_y = lax.rem(my + 1, nmy), lax.rem(my + nmy - 1, nmy)
    right, left = lax.rem(mx + dz, nmx), lax.rem(mx + dz + nmx - 1, nmx)

    own_z, own_x = pl.ds(pl.multiple_of(half * dz, half), half), pl.ds(pl.multiple_of(cx * dz, cx), cx)
    far_z, far_x = pl.ds(pl.multiple_of(half - half * dz, half), half), pl.ds(pl.multiple_of(cx - cx * dz, cx), cx)
    blocks_in = (
        (m_in, mat, ()),
        (e_in, e, (slice(None),)),
        (h_in, h, (slice(None),)),
        (p_in, pq, (slice(None), slice(None))),
    )
    loads = [
        pltpu.make_async_copy(src.at[(*lead, slice(None), own_x)], dst.at[(*lead, own_z)], in_sem.at[i])
        for i, (src, dst, lead) in enumerate(blocks_in)
    ]
    for load in loads:
        load.start()

    barrier = pltpu.get_barrier_semaphore()
    peers = [(up_m, my, dz), (down_m, my, dz), (mx, up_y, dz), (mx, down_y, dz)]
    peers += [(right, my, 1 - dz), (left, my, 1 - dz)]
    for peer in peers:
        pl.semaphore_signal(barrier, inc=1, device_id=peer, device_id_type=MESH)

    one, zero = np.float32(1.0), np.float32(0.0)
    place_x = 2 * mx + dz
    xp, xm = jnp.where(place_x < 2 * nmx - 1, one, zero), jnp.where(place_x > 0, one, zero)
    yp, ym = jnp.where(my < nmy - 1, one, zero), jnp.where(my > 0, one, zero)

    lane = lax.broadcasted_iota(jnp.int32, (cx, cy), 1)
    row = lax.broadcasted_iota(jnp.int32, (cx, cy), 0)
    at_lane0, at_lane_end = lane == 0, lane == cy - 1
    at_row0, at_row_end = row == 0, row == cx - 1
    slab_lane = lax.broadcasted_iota(jnp.int32, (depth, cy), 1)
    slab_row = lax.broadcasted_iota(jnp.int32, (depth, cy), 0)
    slab_lane0, slab_lane_end = slab_lane == 0, slab_lane == cy - 1
    nothing = jnp.zeros((cx, cy), F32)
    slab_nothing = jnp.zeros((depth, cy), F32)

    def to(x, src, dst):
        shift = (dst - src + cy) % cy
        return pltpu.roll(x, shift, axis=1) if not isinstance(shift, int) or shift else x

    def layers(body, carry):
        def some(g, carry):
            for j in range(GROUP):
                carry = body(GROUP * g + j, carry)
            return carry

        return lax.fori_loop(0, depth // GROUP, some, carry)

    def y_next(x):
        return pltpu.roll(x, cy - 1, axis=1)

    def y_last(x):
        return pltpu.roll(x, 1, axis=1)

    def x_next(x):
        return pltpu.roll(x, cx - 1, axis=0)

    def x_last(x):
        return pltpu.roll(x, 1, axis=0)

    def wide(x):
        return jnp.broadcast_to(x, (cx, cy))

    def slot(tile, which):
        return to(tile, which * depth, 0)

    def tile_up(x):
        lanes = lax.broadcasted_iota(jnp.int32, x.shape, 1)
        return jnp.where(lanes == depth - 1, zero, y_next(x)) - x

    def tile_down(x):
        lanes = lax.broadcasted_iota(jnp.int32, x.shape, 1)
        return x - jnp.where(lanes == 0, zero, y_last(x))

    def slab_up(x):
        return jnp.where(slab_row == depth - 1, zero, pltpu.roll(x, depth - 1, axis=0)) - x

    def slab_down(x):
        return x - jnp.where(slab_row == 0, zero, pltpu.roll(x, 1, axis=0))

    def column(x):
        picked = jnp.where(slab_lane == slab_row, jnp.broadcast_to(x, (depth, cy)), slab_nothing)
        return jnp.sum(picked, axis=1, keepdims=True)

    def at_end(x):
        return jnp.where(slab_lane_end, column(x), slab_nothing)

    def at_start(x):
        return jnp.where(slab_lane0, column(x), slab_nothing)

    def poles_of(z, fields):
        keep_d, drive_d, keep_l, drive_l, restore_l, scale = [coef[i, z] for i in range(6)]
        rest = []
        for c, field in enumerate(fields):
            polar, current, drude = pq[0, c, z], pq[1, c, z], pq[2, c, z]
            current_new = keep_l * current + drive_l * field - restore_l * polar
            drude_new = keep_d * drude + drive_d * field
            pq[0, c, z] = polar + DT * current_new
            pq[1, c, z] = current_new
            pq[2, c, z] = drude_new
            rest.append(field - scale * (0.5 * (drude + drude_new) + current_new))
        return rest, scale

    def begin_round(r):
        def layer(z, carry):
            low_tile, high_tile, hx_below, hy_below = carry
            ex, ey, ez = e[0, z], e[1, z], e[2, z]
            exn, eyn = e[0, z + 1], e[1, z + 1]
            dy_ez = jnp.where(at_lane_end, nothing, y_next(ez)) - ez
            dy_ex = jnp.where(at_lane_end, nothing, y_next(ex)) - ex
            dx_ez = jnp.where(at_row_end, nothing, x_next(ez)) - ez
            dx_ey = jnp.where(at_row_end, nothing, x_next(ey)) - ey
            hx = h[0, z] - DT * (dy_ez - (eyn - ey))
            hy = h[1, z] - DT * ((exn - ex) - dx_ez)
            hz = h[2, z] - DT * (dx_ey - dy_ex)
            hp[0, z], hp[1, z], hp[2, z] = hx, hy, hz
            rest, scale = poles_of(z, (ex, ey, ez))
            eb[0, z], eb[1, z], eb[2, z] = rest
            dx_hy = hy - jnp.where(at_row0, nothing, x_last(hy))
            dx_hz = hz - jnp.where(at_row0, nothing, x_last(hz))
            dy_hx = hx - jnp.where(at_lane0, nothing, y_last(hx))
            dy_hz = hz - jnp.where(at_lane0, nothing, y_last(hz))
            px = rest[0] + scale * (dy_hz - (hy - hy_below))
            py = rest[1] + scale * ((hx - hx_below) - dx_hz)
            pz = rest[2] + scale * (dx_hy - dy_hx)
            for i, x in enumerate((hy, hz, px, py, pz, scale)):
                xu[r, i, pl.ds(z, 1), :] = x[cx - 1 : cx]
            for i, x in enumerate((ey, ez, py, pz, scale)):
                xd[r, i, pl.ds(z, 1), :] = x[0:1]
            for i, x in enumerate((ex, ez, px, pz, scale, ey, hy)):
                low_tile = jnp.where(lane == i * depth + z, to(x, 0, i * depth + z), low_tile)
            mixed = jnp.where(at_row0, ez, jnp.where(row == 1, x_last(y_last(ey)), hy))
            for i, x in enumerate((hx, hz, px, py, pz, scale, ey, mixed)):
                high_tile = jnp.where(lane == i * depth + z, to(x, cy - 1, i * depth + z), high_tile)
            return low_tile, high_tile, hx, hy

        low_tile, high_tile, _, _ = layers(layer, (nothing,) * 4)
        yd[r] = low_tile
        yu[r] = high_tile

    def messages(r):
        there = 1 - dz
        table = (
            (yd.at[r], yd_in.at[r, 1], (right, down_y, there)),
            (yu.at[r], yu_in.at[r, 1], (left, up_y, there)),
            (yd.at[r], yd_in.at[r, 2], (left, down_y, there)),
            (yu.at[r], yu_in.at[r, 2], (right, up_y, there)),
            (xu.at[r, pl.ds(0, 6 - r)], xu_in.at[r, pl.ds(0, 6 - r)], (right, my, there)),
            (xd.at[r, pl.ds(0, 5 - r)], xd_in.at[r, pl.ds(0, 5 - r)], (left, my, there)),
            (yd.at[r], yd_in.at[r, 3], (right, my, there)),
            (yd.at[r], yd_in.at[r, 4], (left, my, there)),
            (yd.at[r], yd_in.at[r, 0], (mx, down_y, dz)),
            (yu.at[r], yu_in.at[r, 0], (mx, up_y, dz)),
        )
        copies = [
            pltpu.make_async_remote_copy(
                src_ref=src, dst_ref=dst, send_sem=s_send.at[r, k], recv_sem=s_recv.at[r, k],
                device_id=device, device_id_type=MESH,
            )
            for k, (src, dst, device) in enumerate(table)
        ]
        return copies[:4], copies[4:]

    def electric_at(z, fields, below, hx_ym, hz_ym, rest, scale):
        hx, hy, hz = fields
        dx_hy = hy - jnp.where(at_row0, wide(gx[0, pl.ds(z, 1), :]), x_last(hy))
        dx_hz = hz - jnp.where(at_row0, wide(gx[1, pl.ds(z, 1), :]), x_last(hz))
        dy_hx = hx - jnp.where(at_lane0, to(hx_ym, z, 0), y_last(hx))
        dy_hz = hz - jnp.where(at_lane0, to(hz_ym, z, 0), y_last(hz))
        ex = rest[0] + scale * (dy_hz - (hy - below[1]))
        ey = rest[1] + scale * ((hx - below[0]) - dx_hz)
        ez = rest[2] + scale * (dx_hy - dy_hx)
        return ex, ey, ez

    def here_of(z):
        return jnp.where(exit_ref[0] == z, one, zero)

    def finish_round(r):
        own_low = yd[r]
        top = yd_in[r, 0] * yp
        left_top, right_top = yd_in[r, 1] * (xm * yp), yd_in[r, 2] * (xp * yp)
        left_low, right_low = yd_in[r, 3] * xm, yd_in[r, 4] * xp
        bottom = yu_in[r, 0] * ym
        right_bottom, left_bottom = yu_in[r, 1] * (xp * ym), yu_in[r, 2] * (xm * ym)
        end = cx - 1
        lt = left_top[end : end + 1]
        lt_ex, lt_ez, lt_px, lt_scale, lt_hy = [slot(lt, i) for i in (0, 1, 2, 4, 6)]
        lt_ex2 = left_top[end - 1 : end]
        rb = right_bottom[0:1]
        rb_hx, rb_py, rb_scale, rb_ey, rb_ez = [slot(rb, i) for i in (0, 3, 5, 6, 7)]
        rb_ey2 = slot(right_bottom[1:2], 7)
        lb = left_bottom[end : end + 1]
        lb_hx, lb_hz, lb_hy = [slot(lb, i) for i in (0, 1, 7)]
        rt = right_top[0:1]
        rt_ex, rt_ez, rt_ey = [slot(rt, i) for i in (0, 1, 5)]
        l_ex, l_ez = [slot(left_low[end : end + 1], i) for i in (0, 1)]
        r_ex, r_ez = [slot(right_low[0:1], i) for i in (0, 1)]
        t_ez, t_ey = [slot(top[0:1], i) for i in (1, 5)]
        b_ey, b_ez = slot(bottom[0:1], 6), slot(bottom[0:1], 7)

        corner_hx = (lb_hx - DT * l_ez) * (xm * ym)
        corner_hy = (lb_hy + DT * b_ez) * (xm * ym)
        corner_hz = (lb_hz - DT * b_ey + DT * l_ex) * (xm * ym)
        rb_hx = (rb_hx - DT * r_ez) * (xp * ym)
        lt_hy = (lt_hy + DT * t_ez) * (xm * yp)
        lt_ex_end = at_end(DT * lt_ex)
        more_hy_x = DT * xd[r, 1]
        more_hz_x = lt_ex_end - DT * xd[r, 0]
        hy_x = (xu_in[r, 0] + more_hy_x) * xm
        hz_x = (xu_in[r, 1] + more_hz_x) * xm
        more_hx_y = -DT * slot(own_low, 1)
        more_hz_y = DT * slot(own_low, 0) - jnp.where(at_row_end, DT * rb_ey, nothing)
        hx_y = (bottom + more_hx_y) * ym
        hz_y = (slot(bottom, 1) + more_hz_y) * ym
        gx[0], gx[1] = hy_x, hz_x

        def first(z, carry):
            below, plane, ex_low, ez_low, hx_high, hz_high = carry
            hx, hy, hz = hp[0, z], hp[1, z], hp[2, z]
            hy = hy + jnp.where(at_row_end, wide(xd_in[r, 1, pl.ds(z, 1), :] * (DT * xp)), nothing)
            hz = hz - jnp.where(at_row_end, wide(xd_in[r, 0, pl.ds(z, 1), :] * (DT * xp)), nothing)
            hx = hx - jnp.where(at_lane_end, DT * to(top, depth + z, cy - 1), nothing)
            hz = hz + jnp.where(at_lane_end, DT * to(top, z, cy - 1), nothing)
            h[0, z], h[1, z], h[2, z] = hx, hy, hz
            fields = electric_at(z, (hx, hy, hz), below, hx_y, hz_y, (eb[0, z], eb[1, z], eb[2, z]), coef[5, z])
            ex, ey, ez = fields
            e[0, z], e[1, z], e[2, z] = fields
            rest, _ = poles_of(z, fields)
            eb[0, z], eb[1, z], eb[2, z] = rest
            here = here_of(z)
            plane = (plane[0] + here * ex, plane[1] + here * ey)
            hs[0, pl.ds(z, 1), :] = hy[cx - 1 : cx]
            hs[1, pl.ds(z, 1), :] = hz[cx - 1 : cx]
            es[0, pl.ds(z, 1), :] = ey[0:1]
            es[1, pl.ds(z, 1), :] = ez[0:1]
            ex_low = jnp.where(lane == z, to(ex, 0, z), ex_low)
            ez_low = jnp.where(lane == z, to(ez, 0, z), ez_low)
            hx_high = jnp.where(lane == z, to(hx, cy - 1, z), hx_high)
            hz_high = jnp.where(lane == z, to(hz, cy - 1, z), hz_high)
            return (hx, hy), plane, ex_low, ez_low, hx_high, hz_high

        pair = (nothing, nothing)
        _, plane, ex_low, ez_low, hx_high, hz_high = layers(first, (pair, pair, *pair, *pair))
        ps[2 * r, 0], ps[2 * r, 1] = plane

        more_hx = at_end(-DT * rt_ez)
        more_hz = at_end(DT * rt_ex)
        scale = xd_in[0, 4] * xp
        ey_right = xd_in[r, 2] * xp + scale * (slab_down(more_hx) - more_hz + hs[1])
        ez_right = xd_in[r, 3] * xp + scale * (at_start(rb_hx) - hs[0] - more_hx)
        gx_e = (ey_right, ez_right)

        more_hx = at_end(-DT * lt_ez)
        scale = xu_in[0, 5]
        hz_shift = jnp.where(slab_lane0, column(corner_hz), pltpu.roll(more_hz_x, 1, axis=1))
        ex_left = xu_in[r, 2] + scale * (more_hz_x - hz_shift - slab_down(more_hy_x))
        ey_left = xu_in[r, 3] + scale * (slab_down(more_hx) - (more_hz_x - at_end(DT * lt_ex2)))
        ez_left = xu_in[r, 4] + scale * (more_hy_x - more_hx + at_start(corner_hx))
        lt_more = column(-DT * t_ey - tile_down(DT * t_ez))
        ex_lt = column(lt_px) + column(lt_scale) * (lt_more - hz_x)

        more_hy = jnp.where(at_row_end, DT * rt_ez, nothing)
        more_hz = jnp.where(at_row_end, -DT * rt_ey, nothing)
        scale = slot(top, 4)
        ex_top = slot(top, 2) + scale * (more_hz - hz_high - tile_down(more_hy))
        ez_top = slot(top, 3) + scale * (more_hy - jnp.where(at_row0, lt_hy, nothing) + hx_high)

        more_hy = jnp.where(at_row_end, DT * rb_ez, nothing)
        scale = slot(bottom, 5)
        hz_two = jnp.where(at_row_end, -DT * rb_ey2, nothing)
        ex_bottom = slot(bottom, 2) + scale * (more_hz_y - hz_two - tile_down(more_hy))
        hz_shift = jnp.where(at_row0, wide(corner_hz), x_last(more_hz_y))
        ey_bottom = slot(bottom, 3) + scale * (tile_down(more_hx_y) - (more_hz_y - hz_shift))
        ez_bottom = slot(bottom, 4) + scale * (more_hy - jnp.where(at_row0, corner_hy, nothing) - more_hx_y)
        ey_rb = rb_py + rb_scale * (hz_y[end : end + 1] - DT * r_ex - tile_down(DT * r_ez))

        gx[0] = (hy_x - DT * (slab_up(ex_left) - (es[1] - ez_left))) * xm
        ex_next = jnp.where(slab_lane_end, ex_lt, pltpu.roll(ex_left, cy - 1, axis=1))
        gx[1] = (hz_x - DT * ((es[0] - ey_left) - (ex_next - ex_left))) * xm
        hx_y = (hx_y - DT * ((ez_low - ez_bottom) - tile_up(ey_bottom))) * ym
        ey_next = jnp.where(at_row_end, wide(ey_rb), x_next(ey_bottom))
        hz_y = (hz_y - DT * ((ey_next - ey_bottom) - (ex_low - ex_bottom))) * ym
        hs[0], hs[1] = gx_e

        def second(z, carry):
            below, plane = carry
            ex, ey, ez = e[0, z], e[1, z], e[2, z]
            exn, eyn = e[0, z + 1], e[1, z + 1]
            dy_ez = jnp.where(at_lane_end, to(ez_top, z, cy - 1), y_next(ez)) - ez
            dy_ex = jnp.where(at_lane_end, to(ex_top, z, cy - 1), y_next(ex)) - ex
            dx_ez = jnp.where(at_row_end, wide(hs[1, pl.ds(z, 1), :]), x_next(ez)) - ez
            dx_ey = jnp.where(at_row_end, wide(hs[0, pl.ds(z, 1), :]), x_next(ey)) - ey
            hx = h[0, z] - DT * (dy_ez - (eyn - ey))
            hy = h[1, z] - DT * ((exn - ex) - dx_ez)
            hz = h[2, z] - DT * (dx_ey - dy_ex)
            h[0, z], h[1, z], h[2, z] = hx, hy, hz
            fields = electric_at(z, (hx, hy, hz), below, hx_y, hz_y, (eb[0, z], eb[1, z], eb[2, z]), coef[5, z])
            e[0, z], e[1, z], e[2, z] = fields
            here = here_of(z)
            return (hx, hy), (plane[0] + here * fields[0], plane[1] + here * fields[1])

        _, plane = layers(second, (pair, pair))
        ps[2 * r + 1, 0], ps[2 * r + 1, 1] = plane

    for i in range(3):
        e[i, depth] = nothing

    dzf, mxf, myf = dz.astype(F32), mx.astype(F32), my.astype(F32)
    vrow = lax.broadcasted_iota(jnp.int32, (V, cy), 0).astype(F32) - np.float32(V // 2)
    ypos = lax.broadcasted_iota(jnp.int32, (V, cy), 1).astype(F32) + (myf - np.float32(nmy // 2)) * np.float32(cy)
    size = np.float32(1.0 / math.sqrt(nmy * cy))
    for w in range(W):
        turn = fold(vrow * ypos, np.float32(V * (5 + w)), np.float32(1.0 / (V * (5 + w))))
        bw_high[w, :, 0:cy], bw_low[w, :, 0:cy] = in_two(size * cos_turn(turn))
        bw_high[w, :, cy : 2 * cy], bw_low[w, :, cy : 2 * cy] = in_two(-size * sin_turn(turn))

    r = lax.broadcasted_iota(jnp.int32, (128, 128), 0)
    c = lax.broadcasted_iota(jnp.int32, (128, 128), 1)
    w_r, w_c = (r // 32) % 2, (c // 32) % 2
    own_u = (r % 8).astype(F32) + (mxf * np.float32(8) - np.float32(U // 2))
    inverse = jnp.where(
        w_r == 0,
        jnp.where(dz == 0, np.float32(1.0 / (U * 5)), np.float32(1.0 / (U * 7))),
        jnp.where(dz == 0, np.float32(1.0 / (U * 6)), np.float32(1.0 / (U * 8))),
    )
    quarter = ((r // 16) % 2 - (c // 16) % 2 - r // 64).astype(F32) * np.float32(0.25)
    turn = own_u * (c % 8 + 8 * (c // 64)).astype(F32) * inverse + quarter
    turn = turn - jnp.floor(turn + 0.5)
    same = (w_r == w_c) & ((r // 8) % 2 == (c // 8) % 2)
    tt[0:128, :], tt[128:256, :] = in_two(
        jnp.where(same, np.float32(1.0 / math.sqrt(nmx * 2 * cx)) * cos_turn(turn), zero)
    )

    width = 8 * nmx
    r = lax.broadcasted_iota(jnp.int32, (64, width), 0)
    c = lax.broadcasted_iota(jnp.int32, (64, width), 1)
    own_u = (r % 8).astype(F32) + (mxf * np.float32(8) - np.float32(U // 2))
    parts = U // (2 * cx)
    q = (5 + r // 32).astype(F32) + 2 * dzf
    inverse = jnp.where(
        r // 32 == 0,
        jnp.where(dz == 0, np.float32(1.0 / (parts * 5)), np.float32(1.0 / (parts * 7))),
        jnp.where(dz == 0, np.float32(1.0 / (parts * 6)), np.float32(1.0 / (parts * 8))),
    )
    turn = fold(own_u * ((c // 8).astype(F32) - np.float32(nmx // 2)), q * np.float32(parts), inverse)
    ff[0] = cos_turn(turn)
    ff[1] = -sin_turn(turn)

    for load in loads:
        load.wait()
    pl.semaphore_wait(barrier, len(peers))

    def remote(src, dst, send, recv, device):
        return pltpu.make_async_remote_copy(
            src_ref=src, dst_ref=dst, send_sem=send, recv_sem=recv, device_id=device, device_id_type=MESH
        )

    swaps = [
        remote(
            src.at[(*lead, slice(None), far_x)], dst.at[(*lead, own_z)], swap_send.at[i], swap_recv.at[i], partner
        )
        for i, (src, dst, lead) in enumerate(blocks_in)
    ]
    for swap in swaps:
        swap.start()

    def spread(i):
        for far in (1 << i, -(1 << i)):
            to_x, to_y = lax.rem(mx + far + 2 * nmx, nmx), lax.rem(my + far + 2 * nmy, nmy)
            pl.semaphore_signal(known.at[0, i], inc=1, device_id=(to_x, my, dz), device_id_type=MESH)
            pl.semaphore_signal(known.at[1, i], inc=1, device_id=(mx, to_y, dz), device_id_type=MESH)

    def heard(i):
        pl.semaphore_wait(known.at[0, i], 2)
        pl.semaphore_wait(known.at[1, i], 2)

    spread(0)
    swaps[0].wait()

    def constants(z, carry):
        kind = mat[z]
        for i in range(6):
            t = coef_table[i]
            coef[i, z] = jnp.where(kind < 2, jnp.where(kind == 0, t[0], t[1]), jnp.where(kind == 2, t[2], t[3]))
        return carry

    layers(constants, 0)
    for swap in swaps[1:]:
        swap.wait()

    def two_steps(r, carry):
        begin_round(r)

        @pl.when(r == 0)
        def _():
            diagonal, straight = messages(0)
            for m in straight:
                m.start()
            pl.semaphore_wait(known.at[1, 0], 2)
            for m in diagonal:
                m.start()
            pl.semaphore_wait(known.at[0, 0], 2)
            spread(1)
            for m in straight + diagonal:
                m.wait()

        @pl.when(r == 1)
        def _():
            diagonal, straight = messages(1)
            for m in diagonal + straight:
                m.start()
            heard(1)
            spread(2)
            for m in straight + diagonal:
                m.wait()

        finish_round(r)
        return carry

    lax.fori_loop(0, STEPS // 2, two_steps, 0)

    blocks_out = (
        (e, e_out, (slice(None),)),
        (h, h_out, (slice(None),)),
        (pq, p_out, (slice(None), slice(None))),
    )
    stores = [
        pltpu.make_async_copy(src.at[(*lead, own_z)], dst.at[(*lead, slice(None), own_x)], out_sem.at[i])
        for i, (src, dst, lead) in enumerate(blocks_out)
    ]
    stores += [
        remote(
            src.at[(*lead, far_z)], dst.at[(*lead, slice(None), own_x)], back_send.at[i], back_recv.at[i], partner
        )
        for i, (src, dst, lead) in enumerate(blocks_out)
    ]

    def turned(w, what):
        found = []
        for n in range(1, STEPS + 1):
            found.append(np.float32(what(2 * math.pi * n / (8 + 2 * w))))
        return found

    def along_y(w, carry):
        cos_t, sin_t = turned(w, math.cos), turned(w, math.sin)
        re, im = [], []
        for p in range(2):
            re.append(sum(cos_t[n] * ps[n, p] for n in range(STEPS)))
            im.append(-sum(sin_t[n] * ps[n, p] for n in range(STEPS)))
        re, im = jnp.concatenate(re, 0), jnp.concatenate(im, 0)
        rows = jnp.concatenate([jnp.concatenate([re, -im], 1), jnp.concatenate([im, re], 1)], 0)
        high, low = in_two(rows)
        at = pl.ds(w * 4 * cx, 4 * cx)
        both = matmul(jnp.concatenate([high, low], 0), bw_high[w])
        ct[at, :] = both[0 : 4 * cx] + both[4 * cx : 8 * cx] + matmul(high, bw_low[w])
        return carry

    for w in range(W):
        along_y(w, 0)
    cbuf[...] = jnp.transpose(ct[...]).reshape(nmy, 8, 128)

    def place(j, n):
        return j + 1

    left_half = lax.broadcasted_iota(jnp.int32, (8, 128), 1) < 64
    for m in range(nmy):
        tile = cbuf[m]
        turned_tile = pltpu.roll(tile, 64, axis=1)
        cut[0, m] = jnp.where(left_half, tile, pltpu.roll(turned_tile, 4, axis=0))[0:4]
        cut[1, m] = jnp.where(left_half, turned_tile, pltpu.roll(tile, 4, axis=0))[0:4]

    def share(j, core):
        k = place(j, nmy)
        to_y = lax.rem(my + k, nmy)
        at = remote(
            cut.at[core, to_y], ra.at[dz, k], a_send.at[core, k], a_recv.at[dz, k], (mx, to_y, core)
        )
        return at

    def landing(j, core):
        k = place(j, nmy)
        return remote(cut.at[core, my], ra.at[core, k], a_send.at[core, k], a_recv.at[core, k], (mx, up_y, core))

    by_distance = (10, 6, 2, 14, 9, 7, 11, 5, 8, 3, 13, 1, 15, 4, 12)

    def spread_out(j):
        k = by_distance[j] if nmx == 16 else place(j, nmx)
        return remote(gbuf, gall.at[mx], b_send.at[k], b_recv.at[k], (lax.rem(mx + k, nmx), my, dz))

    pl.semaphore_wait(known.at[1, 2], 2)

    pair = remote(cut.at[1 - dz, my], ra.at[dz, 0], a_send.at[1 - dz, 0], a_recv.at[dz, 0], partner)
    pair_in = remote(cut.at[1 - dz, my], ra.at[1 - dz, 0], a_send.at[1 - dz, 0], a_recv.at[1 - dz, 0], partner)
    pl.semaphore_signal(word, inc=1, device_id=partner, device_id_type=MESH)
    for j in range(nmy - 1):
        share(j, dz).start()
        if j + 1 != nmy // 2:
            share(j, 1 - dz).start()
    pair.start()
    pl.semaphore_wait(word, 1)
    share(nmy // 2 - 1, 1 - dz).start()
    for store in stores:
        store.start()
    ra[dz, 0] = cut[dz, my]
    for core in range(2):
        for j in range(nmy - 1):
            landing(j, core).wait_recv()
    pair_in.wait_recv()
    sums = []
    for core in range(2):
        total = ra[core, 0]
        for k in range(1, nmy):
            total = total + ra[core, k]
        sums.append(total)
    half_row = left_half[0:4]
    top = jnp.where(half_row, sums[0], pltpu.roll(sums[1], 64, axis=1))
    low_rows = jnp.where(half_row, pltpu.roll(sums[0], 64, axis=1), sums[1])
    total = jnp.concatenate([top, low_rows], 0)
    gbuf[...] = total
    gall[mx] = total

    pl.semaphore_wait(known.at[0, 2], 2)
    for j in range(nmx - 1):
        spread_out(j).start()

    for j in range(nmx - 1):
        spread_out(j).wait()

    high, low = in_two(gall[...].reshape(width, 128))
    both = matmul(tt[...], high)
    both = both[0:128] + both[128:256] + matmul(tt[0:128, :], low)
    far = both[0:64] * ff[0] + both[64:128] * ff[1]
    shift = 8
    while shift < width:
        far = far + pltpu.roll(far, shift, axis=1)
        shift *= 2
    far = far.reshape(2, 2, 2, 8, width)
    fbuf[...] = far[..., 0:8]
    last = pltpu.make_async_copy(fbuf, f_out, out_sem.at[3])
    last.start()
    for j in range(nmy - 1):
        for core in range(2):
            share(j, core).wait_send()
    pair.wait_send()
    for store in stores:
        store.wait()
    last.wait()


def hand_over(*refs):
    copies = [pltpu.make_async_copy(a, b, refs[8].at[i]) for i, (a, b) in enumerate(zip(refs[:4], refs[4:8]))]
    for copy in copies:
        copy.start()
    for copy in copies:
        copy.wait()


def body(nmx, nmy, electric, magnetic, poles, material, exit_layer):
    near, cx, cy = material.shape
    depth, mine = 2 * near, cx // 2
    vm = lambda *shape: pltpu.VMEM(shape, F32)
    dma = lambda *shape: pltpu.SemaphoreType.DMA(shape)
    anywhere = pl.BlockSpec(memory_space=pl.ANY)
    field = (3, near, cx, cy)
    held = (3, depth, mine, cy)
    share = (2, 2, 2, U // nmx, V // nmy)
    electric, magnetic, poles, material = (
        pltpu.with_memory_space_constraint(x, pltpu.HBM) for x in (electric, magnetic, poles, material)
    )
    n = STEPS // 2
    outs = pl.pallas_call(
        functools.partial(kernel, nmx, nmy),
        out_shape=(
            jax.ShapeDtypeStruct(field, F32),
            jax.ShapeDtypeStruct(field, F32),
            jax.ShapeDtypeStruct((3, *field), F32),
            jax.ShapeDtypeStruct(share, F32),
        ),
        in_specs=[pl.BlockSpec(memory_space=pltpu.HBM)] * 4 + [pl.BlockSpec(memory_space=pltpu.SMEM)],
        out_specs=[anywhere] * 4,
        scratch_shapes=[
            vm(3, depth + 1, mine, cy), vm(*held), vm(*held), vm(*held), vm(3, *held),
            pltpu.VMEM((depth, mine, cy), jnp.int32), vm(6, depth, mine, cy),
            vm(n, 6, depth, cy), vm(n, 5, depth, cy), vm(n, mine, cy), vm(n, mine, cy),
            vm(n, 6, depth, cy), vm(n, 5, depth, cy), vm(n, 5, mine, cy), vm(n, 3, mine, cy),
            vm(2, depth, cy), vm(2, depth, cy), vm(2, depth, cy), vm(STEPS, 2, mine, cy),
            vm(128, V), *[pltpu.VMEM((W, V, 2 * cy), jnp.bfloat16)] * 2,
            pltpu.VMEM((256, 128), jnp.bfloat16), vm(2, 64, 8 * nmx),
            vm(nmy, 8, 128), vm(2, nmy, 4, 128), vm(2, nmy, 4, 128), vm(8, 128), vm(nmx, 8, 128), vm(*share),
            dma(4), dma(4), dma(4), dma(4), dma(3), dma(3), pltpu.SemaphoreType.REGULAR((2, 3)), pltpu.SemaphoreType.REGULAR,
            dma(n, 10), dma(n, 10), dma(2, nmy), dma(2, nmy), dma(nmx), dma(nmx),
        ],
        compiler_params=pltpu.CompilerParams(collective_id=0, has_side_effects=True, vmem_limit_bytes=24 * 2**20),
    )(electric, magnetic, poles, material, exit_layer)
    shapes = (field, field, (3, *field), share)
    return pl.pallas_call(
        hand_over,
        out_shape=tuple(jax.ShapeDtypeStruct(shape, F32) for shape in shapes),
        in_specs=[anywhere] * 4,
        out_specs=[pl.BlockSpec(memory_space=pltpu.HBM)] * 4,
        scratch_shapes=[dma(4)],
        compiler_params=pltpu.CompilerParams(vmem_limit_bytes=2**20),
    )(*outs)


def solution(mesh):
    nmx, nmy = mesh.shape["mx"], mesh.shape["my"]
    return jax.shard_map(
        functools.partial(body, nmx, nmy),
        mesh=mesh,
        in_specs=(
            P(None, "dz", "mx", "my"),
            P(None, "dz", "mx", "my"),
            P(None, None, "dz", "mx", "my"),
            P("dz", "mx", "my"),
            P(),
        ),
        out_specs=(
            P(None, "dz", "mx", "my"),
            P(None, "dz", "mx", "my"),
            P(None, None, "dz", "mx", "my"),
            P("dz", None, None, "mx", "my"),
        ),
        check_vma=False,
    )
```
